32 devices in a mesh: body: 2 (over core), gx: 4 (over z), gy: 4 (over y, x).
Axes of the slice: x: 2, y: 2, z: 4, core: 2. Of those that a mesh axis runs over, the one named last changes fastest.
Arguments:
- disp: float32 [2, 3, 32, 128, 128], P('body', None, 'gx', 'gy'), may hold values from -4 to 4
- force: float32 [2, 3, 32, 128, 128], P('body', None, 'gx', 'gy'), may hold values from -12 to 12
- kappa: float32 [2, 32, 128, 128], P('body', 'gx', 'gy'), may hold values from 0.05 to 0.5
- sigma: float32 [2, 32, 128, 128], P('body', 'gx', 'gy'), may hold values from 0.2 to 1
- gap0: float32 [32, 128], P(('gx', 'gy')), may hold values from -3 to 3
- pressure: float32 [32, 128], P(('gx', 'gy')), may hold values from 0 to 1
- mortar: float32 [32, 128, 128], P(('gx', 'gy')), may hold values from -0.5 to 0.5
- partner: int32 [32], P(('gx', 'gy')), may hold values from 0 to 7
- active: int32 [32], P(('gx', 'gy')), may hold values 0 or 1
Outputs:
- increment: float32 [2, 3, 32, 128, 128], P('body', None, 'gx', 'gy')
- new_pressure: float32 [32, 128], P(('gx', 'gy'))
The draws below stay inside these ranges and needn't reach their ends.
Inputs may be any that keep to these rules, and one draw needn't show every extreme that they name: partner numbers a master block of the same gy index: gx index times 2 plus the local block. 1 marks a block of the active contact set.
All inputs are finite; a program needn't handle non-finite values.
Results may differ from the reference program's by a relative error of at most 0.00015.
Values sent between devices are 32-bit elements; how exact they have to be, the bound alone decides.
A program may use at most 64 MiB of HBM per device.

```python
import math
import jax
import jax.numpy as jnp
from jax import lax

CX = 8
CY = 32
NZ = 128
SBLK = 128
COMP = 3
CG_ITERS = 2
BLK_DEV = 2
ROWBLK = 8
NBLK = 32
NX = 32
NY = 128
N_GX = 4
N_GY = 4


def plant(values, rng, low, top_value):
    longest = values.shape.index(max(values.shape))
    spots = []
    for shift in (0, 1):
        where = [jax.random.randint(jax.random.fold_in(rng, axis), (), 0, length) for axis, length in enumerate(values.shape)]
        where[longest] = (where[longest] + shift) % values.shape[longest]
        spots.append(tuple(where))
    return values.at[spots[0]].set(low).at[spots[1]].set(top_value)


def level_of(own_key, extent, pieces, low, top_value):
    factor_of = 1.0
    for axis_at, parts in pieces:
        draws = jax.random.uniform(jax.random.fold_in(jax.random.fold_in(own_key, 6), axis_at), (parts,), jnp.float32, low / len(pieces), top_value / len(pieces))
        factor_of = factor_of * jnp.repeat(jnp.exp(draws), extent[axis_at] // parts).reshape((-1,) + (1,) * (len(extent) - 1 - axis_at))
    return factor_of


def scatter_about(stream_key, dims, scale, most, cuts=(), kind=jnp.bfloat16):
    entries = jax.random.normal(stream_key, dims, jnp.float32) * scale
    if len(cuts) > 0:
        entries = level_of(stream_key, dims, cuts, -0.22, 0.18) * entries
    return jnp.clip(entries, min=-most, max=most).astype(kind)


def setup_inputs(seed: int = 0) -> dict:
    streams_of = jax.random.split(jax.random.key(seed), 10)
    return {
        "disp": scatter_about(streams_of[0], (2, COMP, NX, NY, NZ), 0.5, 4.0, ((0, 2), (2, 4), (3, 4)), jnp.float32),
        "force": scatter_about(streams_of[1], (2, COMP, NX, NY, NZ), 2.0, 12.0, ((0, 2), (2, 4), (3, 4)), jnp.float32),
        "kappa": jnp.clip(jnp.exp(math.log(0.5) - 2.3025851 * jax.random.uniform(streams_of[2], (2, NX, NY, NZ), jnp.float32) ** level_of(streams_of[2], (2, NX, NY, NZ), ((0, 2), (1, 4), (2, 4)), -0.2, 0.2)), 0.05, 0.5),
        "sigma": jnp.clip(jnp.exp(math.log(1.0) - 1.609438 * jax.random.uniform(streams_of[3], (2, NX, NY, NZ), jnp.float32) ** level_of(streams_of[3], (2, NX, NY, NZ), ((0, 2), (1, 4), (2, 4)), -0.2, 0.2)), 0.2, 1.0),
        "gap0": scatter_about(streams_of[4], (NBLK, SBLK), 0.5, 3.0, ((0, 16),), jnp.float32),
        "pressure": jnp.clip(1.0 * jax.random.uniform(streams_of[5], (NBLK, SBLK), jnp.float32) ** level_of(streams_of[5], (NBLK, SBLK), ((0, 16),), -0.2, 0.2), 0.0, 1.0),
        "mortar": scatter_about(streams_of[6], (NBLK, SBLK, SBLK), SBLK ** -0.5, 0.5, ((0, 16),), jnp.float32),
        "partner": plant(jax.random.randint(streams_of[7], (NBLK,), 0, ROWBLK), jax.random.fold_in(streams_of[7], 1), 0, ROWBLK - 1).astype(jnp.int32),
        "active": plant((jax.random.randint(streams_of[8], (NBLK,), 0, 2) < 1).astype(jnp.int32), jax.random.fold_in(streams_of[8], 1), 0, 1),
    }


def neighbours():
    result = []
    for first in (-1, 0, 1):
        for second in (-1, 0, 1):
            for third in (-1, 0, 1):
                if first != 0 or second != 0 or third != 0:
                    result.append((first, second, third))
    return result

def apply_stencil(field, padded, kappa, kappa_rim, sigma):
    sizes = field.shape[2:]
    total = sigma[:, None] * field
    for offset in neighbours():
        weight = 0.5 ** (abs(offset[0]) + abs(offset[1]) + abs(offset[2]) - 1)
        lower = [1 + offset[0], 1 + offset[1], 1 + offset[2]]
        bond = 0.5 * (kappa + kappa_rim[:, lower[0]:lower[0] + sizes[0], lower[1]:lower[1] + sizes[1], lower[2]:lower[2] + sizes[2]])
        near = padded[:, :, lower[0]:lower[0] + sizes[0], lower[1]:lower[1] + sizes[1], lower[2]:lower[2] + sizes[2]]
        total = total + weight * bond[:, None] * (field - near)
    return total

def stencil(field, kappa, sigma):
    padded = jnp.pad(field, ((0, 0), (0, 0), (1, 1), (1, 1), (1, 1)))
    kappa_rim = jnp.pad(kappa, ((0, 0), (1, 1), (1, 1), (1, 1)))
    return apply_stencil(field, padded, kappa, kappa_rim, sigma)

def blocks_of(field):
    surface = field[:, 2, :, :, 0]
    surface = surface.reshape(2, N_GX, CX, N_GY, CY).transpose(0, 1, 3, 2, 4)
    return surface.reshape(2, N_GX, N_GY, BLK_DEV, SBLK)

def gap_of(field, partner_grid, mortar_grid):
    surfaces = blocks_of(field)
    master_row = surfaces[1].transpose(1, 0, 2, 3).reshape(N_GY, N_GX * BLK_DEV, SBLK)
    row_index = jnp.arange(N_GY, dtype=jnp.int32)[None, :, None]
    picked = master_row[row_index, partner_grid]
    pulled = jnp.einsum('abcij,abcj->abci', mortar_grid, picked, precision=lax.Precision.HIGHEST)
    return -surfaces[0] - pulled

def spread(traction, partner_grid, mortar_grid):
    pulled = jnp.einsum('abcij,abci->abcj', mortar_grid, traction, precision=lax.Precision.HIGHEST)
    row_index = jnp.arange(N_GY, dtype=jnp.int32)[None, :, None]
    master_row = jnp.zeros((N_GY, N_GX * BLK_DEV, SBLK), jnp.float32).at[row_index, partner_grid].add(-pulled)
    master = master_row.reshape(N_GY, N_GX, BLK_DEV, SBLK).transpose(1, 0, 2, 3)
    both = jnp.stack([-traction, master])
    both = both.reshape(2, N_GX, N_GY, CX, CY).transpose(0, 1, 3, 2, 4)
    return both.reshape(2, NX, NY)

def reference(disp, force, kappa, sigma, gap0, pressure, mortar, partner, active):
    mortar_grid = mortar.reshape(N_GX, N_GY, BLK_DEV, SBLK, SBLK)
    partner_grid = partner.reshape(N_GX, N_GY, BLK_DEV).astype(jnp.int32)
    press = pressure.reshape(N_GX, N_GY, BLK_DEV, SBLK)
    flags = active.reshape(N_GX, N_GY, BLK_DEV, 1).astype(jnp.float32)
    gap = gap0.reshape(N_GX, N_GY, BLK_DEV, SBLK) + gap_of(disp, partner_grid, mortar_grid)
    radius = jnp.sqrt(gap * gap + press * press + 0.01)
    complement = gap + press - radius
    slope_gap = 1.0 - gap / radius
    slope_press = 1.0 - press / radius
    divisor = slope_press + 0.5
    stiffness = flags * slope_gap / divisor
    excess = flags * complement / divisor
    rhs = force - stencil(disp, kappa, sigma)
    rhs = rhs.at[:, 2, :, :, 0].add(spread(flags * press - excess, partner_grid, mortar_grid))

    def operate(field):
        image = stencil(field, kappa, sigma)
        return image.at[:, 2, :, :, 0].add(spread(stiffness * gap_of(field, partner_grid, mortar_grid), partner_grid, mortar_grid))
    increment = jnp.zeros_like(rhs)
    residual, direction = (rhs, rhs)
    norm_now = jnp.sum(residual * residual)
    for step in range(CG_ITERS):
        image = operate(direction)
        alpha = norm_now / jnp.sum(direction * image)
        increment = increment + alpha * direction
        residual = residual - alpha * image
        norm_next = jnp.sum(residual * residual)
        direction = residual + norm_next / norm_now * direction
        norm_now = norm_next
    change = gap_of(increment, partner_grid, mortar_grid)
    new_press = flags * (press - (complement + slope_gap * change) / divisor)
    return (increment, new_press.reshape(NBLK, SBLK))
```

```python
import functools

import jax
import jax.numpy as jnp
from jax import lax
from jax.experimental import pallas as pl
from jax.experimental.pallas import tpu as pltpu
from jax.sharding import PartitionSpec as P

MESH = pl.DeviceIdType.MESH
YB = 8
DIRS = tuple((dx, dy) for dx in (-1, 0, 1) for dy in (-1, 0, 1) if dx != 0 or dy != 0)


def kernel(nb, ngx, ngy, disp, force, kappa, sigma, gap0, press, mortar, partner, active,
           inc_out, np_out, f0, f1, f2, v2, diag, force_v, sigma_v, mort, surf, usend, urecv,
           gsend, grecv, cols, load_sem, hs, hr, ss, sr, us, ur, gs, gr):
    comp, cx, cy, nz = force_v.shape
    bpd, sblk = gap0.shape
    per = sblk // cy
    b = lax.axis_index("body")
    gx = lax.axis_index("gx")
    gy = lax.axis_index("gy")

    loads = [
        pltpu.make_async_copy(disp.at[0], f0.at[pl.ds(0, comp), pl.ds(1, cx), pl.ds(YB, cy)], load_sem.at[0]),
        pltpu.make_async_copy(kappa.at[0], f0.at[comp, pl.ds(1, cx), pl.ds(YB, cy)], load_sem.at[1]),
        pltpu.make_async_copy(mortar, mort, load_sem.at[2]),
        pltpu.make_async_copy(sigma.at[0], sigma_v, load_sem.at[3]),
        pltpu.make_async_copy(force.at[0], force_v, load_sem.at[4]),
    ]
    for load in loads:
        load.start()

    def exists(dx, dy):
        good = jnp.bool_(True)
        if dx < 0:
            good = good & (gx >= 1)
        if dx > 0:
            good = good & (gx < ngx - 1)
        if dy < 0:
            good = good & (gy >= 1)
        if dy > 0:
            good = good & (gy < ngy - 1)
        return good

    for f in (f0, f1, f2):
        for c in range(f.shape[0]):
            for x in (0, cx + 1):
                f[c, x] = jnp.zeros(f.shape[2:], f.dtype)
            for x in range(1, cx + 1):
                f[c, x, YB - 1 : YB] = jnp.zeros((1, nz), f.dtype)
                f[c, x, YB + cy : YB + cy + 1] = jnp.zeros((1, nz), f.dtype)

    row_peers = [(db, k) for db in range(nb) for k in range(ngx) if db or k]
    barrier = pltpu.get_barrier_semaphore()
    for db, k in row_peers:
        pl.semaphore_signal(barrier, inc=1, device_id={"body": lax.rem(b + db, nb), "gx": lax.rem(gx + k, ngx)},
                            device_id_type=MESH)
    for k in range(1, ngy):
        pl.semaphore_signal(barrier, inc=1, device_id={"gy": lax.rem(gy + k, ngy)}, device_id_type=MESH)
    expect = len(row_peers) + ngy - 1
    for dx, dy in DIRS:
        if dx and dy:
            here = exists(dx, dy)
            expect = expect + here.astype(jnp.int32)

            @pl.when(here)
            def _():
                pl.semaphore_signal(barrier, inc=1, device_id={"gx": gx + dx, "gy": gy + dy}, device_id_type=MESH)

    lane = lax.broadcasted_iota(jnp.int32, (sblk, nz), 1)
    eye = lax.broadcasted_iota(jnp.int32, (sblk, nz), 0) == lane
    first_lane = lane == 0
    lane_row = lax.broadcasted_iota(jnp.int32, (cy, nz), 1)
    left_w = jnp.where(lane_row == 0, 0.0, 0.5)
    right_w = jnp.where(lane_row == nz - 1, 0.0, 0.5)

    def to_col(row):
        return jnp.sum(jnp.where(eye, row, 0.0), axis=1, keepdims=True)

    def to_row(col):
        return jnp.sum(jnp.where(eye, col, 0.0), axis=0, keepdims=True)

    def tz(v):
        return v + left_w * pltpu.roll(v, 1, 1) + right_w * pltpu.roll(v, nz - 1, 1)

    def surface_rows(f, r):
        for l in range(bpd):
            block = f[comp - 1, 1 + l * per : 1 + (l + 1) * per, YB : YB + cy, :].reshape(sblk, nz)
            surf[r, b, gx, l : l + 1, :] = to_row(block[:, 0:1])

    pending = []

    def halo_copy(f, r, d, dx, dy, sending):
        def part(delta, size, base):
            if delta == 0:
                return pl.ds(base, size), pl.ds(base, size)
            if delta < 0:
                return pl.ds(base, 1), pl.ds(base + size, 1)
            return pl.ds(base + size - 1, 1), pl.ds(base - 1, 1)
        sx, tx = part(dx, cx, 1)
        sy, ty = part(dy, cy, YB)
        allc = pl.ds(0, f.shape[0])
        return pltpu.make_async_remote_copy(
            src_ref=f.at[allc, sx, sy], dst_ref=f.at[allc, tx, ty], send_sem=hs.at[r, d], recv_sem=hr.at[r, d],
            device_id={"gx": gx + dx, "gy": gy + dy}, device_id_type=MESH)

    def halo_send(f, r):
        for d, (dx, dy) in enumerate(DIRS):
            @pl.when(exists(dx, dy))
            def _():
                halo_copy(f, r, d, dx, dy, True).start()

    def halo_wait(f, r):
        for d, (dx, dy) in enumerate(DIRS):
            @pl.when(exists(-dx, -dy))
            def _():
                halo_copy(f, r, d, dx, dy, False).wait_recv()

    def halo_done(f, r):
        for d, (dx, dy) in enumerate(DIRS):
            @pl.when(exists(dx, dy))
            def _():
                halo_copy(f, r, d, dx, dy, True).wait_send()

    def surf_copy(r, i, db, k, incoming):
        ob, og = lax.rem(b + db, nb), lax.rem(gx + k, ngx)
        wb, wg = (ob, og) if incoming else (b, gx)
        return pltpu.make_async_remote_copy(
            src_ref=surf.at[r, wb, wg], dst_ref=surf.at[r, wb, wg], send_sem=ss.at[r, i],
            recv_sem=sr.at[r, wb * ngx + wg], device_id={"body": ob, "gx": og}, device_id_type=MESH)

    def surf_send(r):
        for i, (db, k) in enumerate(row_peers):
            surf_copy(r, i, db, k, False).start()

    def surf_wait(r):
        for i, (db, k) in enumerate(row_peers):
            surf_copy(r, i, db, k, True).wait_recv()

    def u_copy(r, k, incoming):
        og = lax.rem(gx + k, ngx)
        return pltpu.make_async_remote_copy(
            src_ref=usend.at[r, og], dst_ref=urecv.at[r, og if incoming else gx], send_sem=us.at[r, k],
            recv_sem=ur.at[r, og if incoming else gx], device_id={"gx": og}, device_id_type=MESH)

    def g_copy(s, k, incoming):
        og = lax.rem(gy + k, ngy)
        w = og if incoming else gy
        return pltpu.make_async_remote_copy(
            src_ref=grecv.at[s, w], dst_ref=grecv.at[s, w], send_sem=gs.at[s, k], recv_sem=gr.at[s, w],
            device_id={"gy": og}, device_id_type=MESH)

    def g_send(s, r):
        total = surf[r, 0, 0]
        for w in range(1, nb * ngx):
            total = total + surf[r, w // ngx, w % ngx]
        grecv[s, gy] = total
        for k in range(1, ngy):
            g_copy(s, k, False).start()

    def g_take(s):
        for k in range(1, ngy):
            g_copy(s, k, True).wait_recv()
        total = grecv[s, 0]
        for w in range(1, ngy):
            total = total + grecv[s, w]
        norm = jnp.sum(total[bpd : bpd + 1, :], axis=1, keepdims=True)
        product = jnp.sum(total[bpd + 1 : bpd + 2, :], axis=1, keepdims=True)
        return norm, product

    def b_of(r, l):
        picked = jnp.zeros((1, sblk), jnp.float32)
        for g in range(ngx):
            for q in range(bpd):
                picked = picked + jnp.where(partner[l] == g * bpd + q, surf[r, 1, g, q : q + 1, :], 0.0)
        slave = surf[r, 0, gx, l : l + 1, :]
        return -jnp.sum(mort[l] * picked + jnp.where(eye, slave, 0.0), axis=1, keepdims=True)

    def u_start(r):
        pulled = [jnp.sum(mort[l] * cols[5, l], axis=0, keepdims=True) for l in range(bpd)]
        for g in range(ngx):
            for q in range(bpd):
                row = jnp.zeros((1, sblk), jnp.float32)
                for l in range(bpd):
                    row = row + jnp.where(partner[l] == g * bpd + q, pulled[l], 0.0)
                usend[r, g, q : q + 1, :] = row

        @pl.when(b == 1)
        def _():
            for k in range(1, ngx):
                u_copy(r, k, False).start()

    def u_finish(r, f, x0, y0):
        def add(l, col):
            xs = slice(x0 + l * per, x0 + (l + 1) * per)
            block = f[comp - 1, xs, y0 : y0 + cy, :].reshape(sblk, nz)
            f[comp - 1, xs, y0 : y0 + cy, :] = (block - jnp.where(first_lane, col, 0.0)).reshape(per, cy, nz)

        @pl.when(b == 0)
        def _():
            for l in range(bpd):
                add(l, cols[5, l])

        @pl.when(b == 1)
        def _():
            for k in range(1, ngx):
                u_copy(r, k, True).wait_recv()
            urecv[r, gx] = usend[r, gx]
            for l in range(bpd):
                row = urecv[r, 0, l : l + 1, :]
                for g in range(1, ngx):
                    row = row + urecv[r, g, l : l + 1, :]
                add(l, to_col(row))

    def apply(f, emit):
        @pl.loop(0, comp)
        def _(c):
            window = []
            for x in range(cx + 2):
                kap = [f0[comp, x, YB + s : YB + s + cy, :] for s in (-1, 0, 1)]
                val = [f[c, x, YB + s : YB + s + cy, :] for s in (-1, 0, 1)]
                window.append((val[1] + 0.5 * (val[0] + val[2]),
                               kap[1] * val[1] + 0.5 * (kap[0] * val[0] + kap[2] * val[2])))
                if x >= 2:
                    p = window[x - 1][0] + 0.5 * (window[x - 2][0] + window[x][0])
                    q = window[x - 1][1] + 0.5 * (window[x - 2][1] + window[x][1])
                    k0 = f0[comp, x - 1, YB : YB + cy, :]
                    v0 = f[c, x - 1, YB : YB + cy, :]
                    emit(c, x - 2, diag[x - 2] * v0 - k0 * tz(p) - tz(q))

    loads[0].wait()
    loads[1].wait()
    surf[0, b, gx] = jnp.zeros(surf.shape[3:], jnp.float32)
    surface_rows(f0, 0)
    usend[...] = jnp.zeros(usend.shape, jnp.float32)
    pl.semaphore_wait(barrier, expect)

    surf_send(0)
    halo_send(f0, 0)
    for load in loads[2:]:
        load.wait()
    surf_wait(0)
    for l in range(bpd):
        gap = to_col(gap0[l : l + 1, :]) + b_of(0, l)
        prs = to_col(press[l : l + 1, :])
        radius = jnp.sqrt(gap * gap + prs * prs + 0.01)
        complement = gap + prs - radius
        slope_gap = 1.0 - gap / radius
        divisor = (1.0 - prs / radius) + 0.5
        flag = active[l].astype(jnp.float32)
        cols[0, l] = flag * slope_gap / divisor
        cols[1, l] = complement / divisor
        cols[2, l] = slope_gap / divisor
        cols[5, l] = flag * prs - flag * complement / divisor
    u_start(0)
    halo_wait(f0, 0)
    window = []
    for x in range(cx + 2):
        kap = [f0[comp, x, YB + s : YB + s + cy, :] for s in (-1, 0, 1)]
        window.append(kap[1] + 0.5 * (kap[0] + kap[2]))
        if x >= 2:
            p = window[x - 1] + 0.5 * (window[x - 2] + window[x])
            diag[x - 2] = sigma_v[x - 2] + 8.0 * f0[comp, x - 1, YB : YB + cy, :] + tz(p)

    def emit_rhs(c, x, val):
        f1[c, 1 + x, YB : YB + cy, :] = force_v[c, x] - val

    apply(f0, emit_rhs)
    u_finish(0, f1, 1, YB)

    surf[1, b, gx] = jnp.zeros(surf.shape[3:], jnp.float32)
    surface_rows(f1, 1)
    surf_send(1)
    halo_send(f1, 1)
    surf_wait(1)
    for l in range(bpd):
        gap = b_of(1, l)
        cols[3, l] = gap
        cols[5, l] = cols[0, l] * gap
    u_start(1)
    halo_wait(f1, 1)

    def emit_v1(c, x, val):
        f2[c, 1 + x, YB : YB + cy, :] = val

    apply(f1, emit_v1)
    u_finish(1, f2, 1, YB)

    def sums(left, right):
        norm = jnp.zeros((cy, nz), jnp.float32)
        product = jnp.zeros((cy, nz), jnp.float32)
        for c in range(comp):
            for x in range(cx):
                a, m = left(c, x), right(c, x)
                norm = norm + a * a
                product = product + a * m
        return jnp.sum(norm, axis=0, keepdims=True), jnp.sum(product, axis=0, keepdims=True)

    def r0_of(c, x):
        return f1[c, 1 + x, YB : YB + cy, :]

    def v1_of(c, x):
        return f2[c, 1 + x, YB : YB + cy, :]

    surf[2, b, gx] = jnp.zeros(surf.shape[3:], jnp.float32)
    norm, product = sums(r0_of, v1_of)
    surf[2, b, gx, bpd : bpd + 1, :] = norm
    surf[2, b, gx, bpd + 1 : bpd + 2, :] = product
    surface_rows(f2, 2)
    surf_send(2)
    halo_send(f2, 2)
    surf_wait(2)
    g_send(0, 2)
    for l in range(bpd):
        gap = b_of(2, l)
        cols[4, l] = gap
        cols[5, l] = cols[0, l] * gap
    u_start(2)
    halo_wait(f2, 2)

    def emit_v2(c, x, val):
        v2[c, x] = val

    apply(f2, emit_v2)
    u_finish(2, v2, 0, 0)
    norm0, product0 = g_take(0)
    alpha0 = norm0 / product0

    norm, product = sums(lambda c, x: r0_of(c, x) - alpha0 * v1_of(c, x),
                         lambda c, x: v1_of(c, x) - alpha0 * v2[c, x])
    surf[3, b, gx] = jnp.zeros(surf.shape[3:], jnp.float32)
    surf[3, b, gx, bpd : bpd + 1, :] = norm
    surf[3, b, gx, bpd + 1 : bpd + 2, :] = product
    surf_send(3)
    surf_wait(3)
    g_send(1, 3)
    norm1, product1 = g_take(1)
    ratio = norm1 / norm0
    alpha1 = norm1 / (product1 - ratio * norm1 / alpha0)
    coef_r = alpha0 + alpha1 * (1.0 + ratio)
    coef_v = -alpha1 * alpha0
    for c in range(comp):
        for x in range(cx):
            inc_out[0, c, x] = coef_r * r0_of(c, x) + coef_v * v1_of(c, x)
    for l in range(bpd):
        change = coef_r * cols[3, l] + coef_v * cols[4, l]
        flag = active[l].astype(jnp.float32)
        step = to_row(cols[1, l] + cols[2, l] * change)
        np_out[l : l + 1, :] = flag * (press[l : l + 1, :] - step)

    for r, f in enumerate((f0, f1, f2)):
        halo_done(f, r)
    for r in range(4):
        for i, (db, k) in enumerate(row_peers):
            surf_copy(r, i, db, k, False).wait_send()
    for s in range(2):
        for k in range(1, ngy):
            g_copy(s, k, False).wait_send()

    @pl.when(b == 1)
    def _():
        for r in range(3):
            for k in range(1, ngx):
                u_copy(r, k, False).wait_send()


def on_device(disp, force, kappa, sigma, gap0, pressure, mortar, partner, active):
    nb, ngx, ngy = (lax.axis_size(a) for a in ("body", "gx", "gy"))
    _, comp, cx, cy, nz = disp.shape
    bpd, sblk, _ = mortar.shape
    f32 = jnp.float32
    any_spec = pl.BlockSpec(memory_space=pl.ANY)
    vmem = pl.BlockSpec(memory_space=pltpu.VMEM)
    smem = pl.BlockSpec(memory_space=pltpu.SMEM)
    rows = cy + 2 * YB
    dma = pltpu.SemaphoreType.DMA
    return pl.pallas_call(
        functools.partial(kernel, nb, ngx, ngy),
        out_shape=(jax.ShapeDtypeStruct(disp.shape, f32), jax.ShapeDtypeStruct(gap0.shape, f32)),
        in_specs=[any_spec, any_spec, any_spec, any_spec, vmem, vmem, any_spec, smem, smem],
        out_specs=(vmem, vmem),
        scratch_shapes=[
            pltpu.VMEM((comp + 1, cx + 2, rows, nz), f32),
            pltpu.VMEM((comp, cx + 2, rows, nz), f32),
            pltpu.VMEM((comp, cx + 2, rows, nz), f32),
            pltpu.VMEM((comp, cx, cy, nz), f32),
            pltpu.VMEM((cx, cy, nz), f32),
            pltpu.VMEM((comp, cx, cy, nz), f32),
            pltpu.VMEM((cx, cy, nz), f32),
            pltpu.VMEM((bpd, sblk, sblk), f32),
            pltpu.VMEM((4, nb, ngx, 8, sblk), f32),
            pltpu.VMEM((3, ngx, 8, sblk), f32),
            pltpu.VMEM((3, ngx, 8, sblk), f32),
            pltpu.VMEM((8, sblk), f32),
            pltpu.VMEM((2, ngy, 8, sblk), f32),
            pltpu.VMEM((6, bpd, sblk, 1), f32),
            dma((5,)),
            dma((3, len(DIRS))), dma((3, len(DIRS))),
            dma((4, nb * ngx)), dma((4, nb * ngx)),
            dma((3, ngx)), dma((3, ngx)),
            dma((2, ngy)), dma((2, ngy)),
        ],
        compiler_params=pltpu.CompilerParams(collective_id=0, has_side_effects=True,
                                             vmem_limit_bytes=60 * 1024 * 1024),
        name="newton_step",
    )(disp, force, kappa, sigma, gap0, pressure, mortar, partner, active)


def solution(mesh):
    placed = (
        P("body", None, "gx", "gy", None),
        P("body", None, "gx", "gy", None),
        P("body", "gx", "gy", None),
        P("body", "gx", "gy", None),
        P(("gx", "gy"), None),
        P(("gx", "gy"), None),
        P(("gx", "gy"), None, None),
        P(("gx", "gy")),
        P(("gx", "gy")),
    )
    return jax.shard_map(
        on_device,
        mesh=mesh,
        in_specs=placed,
        out_specs=(P("body", None, "gx", "gy", None), P(("gx", "gy"), None)),
        check_vma=False,
    )
```

```python
import functools

import jax
import jax.numpy as jnp
from jax import lax
from jax.experimental import pallas as pl
from jax.experimental.pallas import tpu as pltpu
from jax.sharding import PartitionSpec as P

MESH = pl.DeviceIdType.MESH
YB = 8
DIRS = tuple((dx, dy) for dx in (-1, 0, 1) for dy in (-1, 0, 1) if dx != 0 or dy != 0)


def kernel(nb, ngx, ngy, disp, force, kappa, sigma, gap0_in, press_in, mortar, partner_in, active_in,
           inc_out, np_out, gap0, press, partner, active, f0, f1, f2, v2, diag, force_v, sigma_v, mort, surf, usend, urecv,
           grecv, final, cols, load_sem, hs, hr, ss, sr, us, ur, gs, gr, fs, fr):
    comp, cx, cy, nz = force_v.shape
    bpd, sblk = gap0.shape
    per = sblk // cy
    b = lax.axis_index("body")
    gx = lax.axis_index("gx")
    gy = lax.axis_index("gy")

    loads = [
        pltpu.make_async_copy(disp.at[0], f0.at[pl.ds(0, comp), pl.ds(1, cx), pl.ds(YB, cy)], load_sem.at[0]),
        pltpu.make_async_copy(kappa.at[0], f0.at[comp, pl.ds(1, cx), pl.ds(YB, cy)], load_sem.at[1]),
        pltpu.make_async_copy(mortar, mort, load_sem.at[2]),
        pltpu.make_async_copy(sigma.at[0], sigma_v, load_sem.at[3]),
        pltpu.make_async_copy(force.at[0], force_v, load_sem.at[4]),
        pltpu.make_async_copy(gap0_in, gap0, load_sem.at[5]),
        pltpu.make_async_copy(press_in, press, load_sem.at[6]),
        pltpu.make_async_copy(partner_in, partner, load_sem.at[7]),
        pltpu.make_async_copy(active_in, active, load_sem.at[8]),
    ]
    for load in loads:
        load.start()

    def exists(dx, dy):
        good = jnp.bool_(True)
        if dx < 0:
            good = good & (gx >= 1)
        if dx > 0:
            good = good & (gx < ngx - 1)
        if dy < 0:
            good = good & (gy >= 1)
        if dy > 0:
            good = good & (gy < ngy - 1)
        return good

    row_peers = [(db, k) for db in range(nb) for k in range(ngx) if db or k]
    barrier = pltpu.get_barrier_semaphore()
    for db, k in row_peers:
        pl.semaphore_signal(barrier, inc=1, device_id={"body": lax.rem(b + db, nb), "gx": lax.rem(gx + k, ngx)},
                            device_id_type=MESH)
    for k in range(1, ngy):
        pl.semaphore_signal(barrier, inc=1, device_id={"gy": lax.rem(gy + k, ngy)}, device_id_type=MESH)
    expect = len(row_peers) + ngy - 1
    for dx, dy in DIRS:
        if dx and dy:
            here = exists(dx, dy)
            expect = expect + here.astype(jnp.int32)

            @pl.when(here)
            def _():
                pl.semaphore_signal(barrier, inc=1, device_id={"gx": gx + dx, "gy": gy + dy}, device_id_type=MESH)

    for side, x in ((-1, 0), (1, cx + 1)):
        @pl.when(jnp.logical_not(exists(side, 0)))
        def _():
            for f in (f0, f1, f2):
                for c in range(f.shape[0]):
                    f[c, x, YB - 1 : YB] = jnp.zeros((1, nz), f.dtype)
                    f[c, x, YB : YB + cy] = jnp.zeros((cy, nz), f.dtype)
                    f[c, x, YB + cy : YB + cy + 1] = jnp.zeros((1, nz), f.dtype)
    for side, y in ((-1, YB - 1), (1, YB + cy)):
        @pl.when(jnp.logical_not(exists(0, side)))
        def _():
            for f in (f0, f1, f2):
                for c in range(f.shape[0]):
                    for x in range(cx + 2):
                        f[c, x, y : y + 1] = jnp.zeros((1, nz), f.dtype)

    lane = lax.broadcasted_iota(jnp.int32, (sblk, nz), 1)
    eye = lax.broadcasted_iota(jnp.int32, (sblk, nz), 0) == lane
    first_lane = lane == 0
    lane_row = lax.broadcasted_iota(jnp.int32, (cy, nz), 1)
    left_w = jnp.where(lane_row == 0, 0.0, 0.5)
    right_w = jnp.where(lane_row == nz - 1, 0.0, 0.5)

    def to_col(row):
        return jnp.sum(jnp.where(eye, row, 0.0), axis=1, keepdims=True)

    def to_row(col):
        return jnp.sum(jnp.where(eye, col, 0.0), axis=0, keepdims=True)

    def tz(v):
        return v + left_w * pltpu.roll(v, 1, 1) + right_w * pltpu.roll(v, nz - 1, 1)

    def surface_rows(f, r):
        for l in range(bpd):
            block = f[comp - 1, 1 + l * per : 1 + (l + 1) * per, YB : YB + cy, :].reshape(sblk, nz)
            surf[r, b, gx, l : l + 1, :] = to_row(block[:, 0:1])

    pending = []

    def halo_copy(f, r, d, dx, dy, sending):
        def part(delta, size, base):
            if delta == 0:
                return pl.ds(base, size), pl.ds(base, size)
            if delta < 0:
                return pl.ds(base, 1), pl.ds(base + size, 1)
            return pl.ds(base + size - 1, 1), pl.ds(base - 1, 1)
        sx, tx = part(dx, cx, 1)
        sy, ty = part(dy, cy, YB)
        allc = pl.ds(0, f.shape[0])
        return pltpu.make_async_remote_copy(
            src_ref=f.at[allc, sx, sy], dst_ref=f.at[allc, tx, ty], send_sem=hs.at[r, d], recv_sem=hr.at[r, d],
            device_id={"gx": gx + dx, "gy": gy + dy}, device_id_type=MESH)

    def halo_send(f, r):
        for d, (dx, dy) in enumerate(DIRS):
            @pl.when(exists(dx, dy))
            def _():
                halo_copy(f, r, d, dx, dy, True).start()

    def halo_wait(f, r):
        for d, (dx, dy) in enumerate(DIRS):
            @pl.when(exists(-dx, -dy))
            def _():
                halo_copy(f, r, d, dx, dy, False).wait_recv()

    def halo_done(f, r):
        for d, (dx, dy) in enumerate(DIRS):
            @pl.when(exists(dx, dy))
            def _():
                halo_copy(f, r, d, dx, dy, True).wait_send()

    def surf_copy(r, i, db, k, incoming):
        ob, og = lax.rem(b + db, nb), lax.rem(gx + k, ngx)
        wb, wg = (ob, og) if incoming else (b, gx)
        return pltpu.make_async_remote_copy(
            src_ref=surf.at[r, wb, wg], dst_ref=surf.at[r, wb, wg], send_sem=ss.at[r, i],
            recv_sem=sr.at[r, wb * ngx + wg], device_id={"body": ob, "gx": og}, device_id_type=MESH)

    def surf_each(r, incoming, act):
        for i, (db, k) in enumerate(row_peers):
            def go():
                act(surf_copy(r, i, db, k, incoming))
            if r >= 2 or (db == 1 and k == 0):
                go()
            else:
                origin = lax.rem(b + db, nb) if incoming else b
                pl.when(origin == 1)(go)

    def surf_send(r):
        surf_each(r, False, lambda copy: copy.start())

    def surf_wait(r):
        surf_each(r, True, lambda copy: copy.wait_recv())

    def u_copy(r, k, incoming):
        og = lax.rem(gx + k, ngx)
        return pltpu.make_async_remote_copy(
            src_ref=usend.at[r, og], dst_ref=urecv.at[r, og if incoming else gx], send_sem=us.at[r, k],
            recv_sem=ur.at[r, og if incoming else gx], device_id={"gx": og}, device_id_type=MESH)

    def g_copy(s, k, incoming):
        og = lax.rem(gy + k, ngy)
        w = og if incoming else gy
        return pltpu.make_async_remote_copy(
            src_ref=grecv.at[s, w], dst_ref=grecv.at[s, w], send_sem=gs.at[s, k], recv_sem=gr.at[s, w],
            device_id={"gy": og}, device_id_type=MESH)

    def scalars(total):
        return (jnp.sum(total[0:1, :], axis=1, keepdims=True), jnp.sum(total[1:2, :], axis=1, keepdims=True))

    def g_send():
        total = surf[2, 0, 0, bpd : bpd + 2, :]
        for w in range(1, nb * ngx):
            total = total + surf[2, w // ngx, w % ngx, bpd : bpd + 2, :]
        grecv[0, gy] = total
        for k in range(1, ngy):
            g_copy(0, k, False).start()

    def g_take():
        for k in range(1, ngy):
            g_copy(0, k, True).wait_recv()
        total = grecv[0, 0]
        for w in range(1, ngy):
            total = total + grecv[0, w]
        return scalars(total)

    count = nb * ngx * ngy
    me = (b * ngx + gx) * ngy + gy

    def each_peer(act):
        if count <= 64:
            for k in range(1, count):
                act(k)
        else:
            pl.loop(1, count)(act)

    def final_copy(k, incoming):
        other = lax.rem(me + k, count)
        w = other if incoming else me
        return pltpu.make_async_remote_copy(
            src_ref=final.at[w], dst_ref=final.at[w], send_sem=fs.at[k], recv_sem=fr.at[w],
            device_id={"body": other // (ngx * ngy), "gx": lax.rem(other // ngy, ngx), "gy": lax.rem(other, ngy)},
            device_id_type=MESH)

    def b_of(r, l):
        picked = jnp.zeros((1, sblk), jnp.float32)
        for g in range(ngx):
            for q in range(bpd):
                picked = picked + jnp.where(partner[l] == g * bpd + q, surf[r, 1, g, q : q + 1, :], 0.0)
        slave = surf[r, 0, gx, l : l + 1, :]
        return -jnp.sum(mort[l] * picked + jnp.where(eye, slave, 0.0), axis=1, keepdims=True)

    def u_start(r):
        pulled = [jnp.sum(mort[l] * cols[5, l], axis=0, keepdims=True) for l in range(bpd)]
        for g in range(ngx):
            for q in range(bpd):
                row = jnp.zeros((1, sblk), jnp.float32)
                for l in range(bpd):
                    row = row + jnp.where(partner[l] == g * bpd + q, pulled[l], 0.0)
                usend[r, g, q : q + 1, :] = row

        @pl.when(b == 1)
        def _():
            for k in range(1, ngx):
                u_copy(r, k, False).start()

    def u_finish(r, f, x0, y0):
        def add(l, col):
            if f is None:
                return
            xs = slice(x0 + l * per, x0 + (l + 1) * per)
            block = f[comp - 1, xs, y0 : y0 + cy, :].reshape(sblk, nz)
            f[comp - 1, xs, y0 : y0 + cy, :] = (block - jnp.where(first_lane, col, 0.0)).reshape(per, cy, nz)

        @pl.when(b == 0)
        def _():
            for l in range(bpd):
                cols[6, l] = cols[5, l]
                add(l, cols[5, l])

        @pl.when(b == 1)
        def _():
            for k in range(1, ngx):
                u_copy(r, k, True).wait_recv()
            urecv[r, gx] = usend[r, gx]
            for l in range(bpd):
                row = urecv[r, 0, l : l + 1, :]
                for g in range(1, ngx):
                    row = row + urecv[r, g, l : l + 1, :]
                col = to_col(row)
                cols[6, l] = col
                add(l, col)

    def apply(f, emit):
        @pl.loop(0, comp)
        def _(c):
            window = []
            for x in range(cx + 2):
                kap = [f0[comp, x, YB + s : YB + s + cy, :] for s in (-1, 0, 1)]
                val = [f[c, x, YB + s : YB + s + cy, :] for s in (-1, 0, 1)]
                window.append((val[1] + 0.5 * (val[0] + val[2]),
                               kap[1] * val[1] + 0.5 * (kap[0] * val[0] + kap[2] * val[2])))
                if x >= 2:
                    p = window[x - 1][0] + 0.5 * (window[x - 2][0] + window[x][0])
                    q = window[x - 1][1] + 0.5 * (window[x - 2][1] + window[x][1])
                    k0 = f0[comp, x - 1, YB : YB + cy, :]
                    v0 = f[c, x - 1, YB : YB + cy, :]
                    emit(c, x - 2, diag[x - 2] * v0 - k0 * tz(p) - tz(q))

    loads[0].wait()
    loads[1].wait()
    surf[0, b, gx] = jnp.zeros(surf.shape[3:], jnp.float32)
    surface_rows(f0, 0)
    pl.semaphore_wait(barrier, expect)

    surf_send(0)
    halo_send(f0, 0)
    for load in loads[2:]:
        load.wait()
    surf_wait(0)
    for l in range(bpd):
        gap = to_col(gap0[l : l + 1, :]) + b_of(0, l)
        prs = to_col(press[l : l + 1, :])
        radius = jnp.sqrt(gap * gap + prs * prs + 0.01)
        complement = gap + prs - radius
        slope_gap = 1.0 - gap / radius
        divisor = (1.0 - prs / radius) + 0.5
        flag = active[l].astype(jnp.float32)
        cols[0, l] = flag * slope_gap / divisor
        cols[1, l] = complement / divisor
        cols[2, l] = slope_gap / divisor
        cols[5, l] = flag * prs - flag * complement / divisor
    u_start(0)
    halo_wait(f0, 0)
    window = []
    for x in range(cx + 2):
        kap = [f0[comp, x, YB + s : YB + s + cy, :] for s in (-1, 0, 1)]
        window.append(kap[1] + 0.5 * (kap[0] + kap[2]))
        if x >= 2:
            p = window[x - 1] + 0.5 * (window[x - 2] + window[x])
            diag[x - 2] = sigma_v[x - 2] + 8.0 * f0[comp, x - 1, YB : YB + cy, :] + tz(p)

    def emit_rhs(c, x, val):
        f1[c, 1 + x, YB : YB + cy, :] = force_v[c, x] - val

    apply(f0, emit_rhs)
    u_finish(0, f1, 1, YB)

    surf[1, b, gx] = jnp.zeros(surf.shape[3:], jnp.float32)
    surface_rows(f1, 1)
    surf_send(1)
    halo_send(f1, 1)
    surf_wait(1)
    for l in range(bpd):
        gap = b_of(1, l)
        cols[3, l] = gap
        cols[5, l] = cols[0, l] * gap
    u_start(1)
    halo_wait(f1, 1)

    def emit_v1(c, x, val):
        f2[c, 1 + x, YB : YB + cy, :] = val

    apply(f1, emit_v1)

    def sum_of(left, right):
        total = jnp.zeros((cy, nz), jnp.float32)
        for c in range(comp):
            for x in range(cx):
                total = total + left(c, x) * right(c, x)
        return jnp.sum(total, axis=0, keepdims=True)

    def surface_col(value, l):
        return jnp.concatenate([value(comp - 1, l * per + i) for i in range(per)], axis=0)

    def surface_sum(left, right_cols):
        total = jnp.zeros((1, nz), jnp.float32)
        for l in range(bpd):
            term = jnp.where(first_lane, surface_col(left, l) * right_cols[l], 0.0)
            total = total + jnp.sum(term, axis=0, keepdims=True)
        return total

    def r0_of(c, x):
        return f1[c, 1 + x, YB : YB + cy, :]

    def v1_of(c, x):
        return f2[c, 1 + x, YB : YB + cy, :]

    norm = sum_of(r0_of, r0_of)
    product = sum_of(r0_of, v1_of)
    u_finish(1, f2, 1, YB)
    product = product - surface_sum(r0_of, [cols[6, l] for l in range(bpd)])

    surf[2, b, gx] = jnp.zeros(surf.shape[3:], jnp.float32)
    surf[2, b, gx, bpd : bpd + 1, :] = norm
    surf[2, b, gx, bpd + 1 : bpd + 2, :] = product
    surface_rows(f2, 2)
    surf_send(2)
    halo_send(f2, 2)
    surf_wait(2)
    g_send()
    for l in range(bpd):
        gap = b_of(2, l)
        cols[4, l] = gap
        cols[5, l] = cols[0, l] * gap
    u_start(2)
    halo_wait(f2, 2)

    def emit_v2(c, x, val):
        v2[c, x] = val

    apply(f2, emit_v2)
    norm0, product0 = g_take()
    alpha0 = norm0 / product0

    def r1_of(c, x):
        return r0_of(c, x) - alpha0 * v1_of(c, x)

    norm = sum_of(r1_of, r1_of)
    product = sum_of(r1_of, lambda c, x: v1_of(c, x) - alpha0 * v2[c, x])
    u_finish(2, None, 0, 0)
    product = product + alpha0 * surface_sum(r1_of, [cols[6, l] for l in range(bpd)])
    final[me, 0:1, :] = norm
    final[me, 1:2, :] = product
    each_peer(lambda k: final_copy(k, False).start())
    each_peer(lambda k: final_copy(k, True).wait_recv())
    norm1, product1 = scalars(lax.fori_loop(1, count, lambda w, t: t + final[w], final[0], unroll=count <= 64))
    ratio = norm1 / norm0
    alpha1 = norm1 / (product1 - ratio * norm1 / alpha0)
    coef_r = alpha0 + alpha1 * (1.0 + ratio)
    coef_v = -alpha1 * alpha0
    for c in range(comp):
        for x in range(cx):
            inc_out[0, c, x] = coef_r * r0_of(c, x) + coef_v * v1_of(c, x)
    for l in range(bpd):
        change = coef_r * cols[3, l] + coef_v * cols[4, l]
        flag = active[l].astype(jnp.float32)
        step = to_row(cols[1, l] + cols[2, l] * change)
        np_out[l : l + 1, :] = flag * (press[l : l + 1, :] - step)

    for r, f in enumerate((f0, f1, f2)):
        halo_done(f, r)
    for r in range(3):
        surf_each(r, False, lambda copy: copy.wait_send())
    for k in range(1, ngy):
        g_copy(0, k, False).wait_send()
    each_peer(lambda k: final_copy(k, False).wait_send())

    @pl.when(b == 1)
    def _():
        for r in range(3):
            for k in range(1, ngx):
                u_copy(r, k, False).wait_send()


def on_device(disp, force, kappa, sigma, gap0, pressure, mortar, partner, active):
    nb, ngx, ngy = (lax.axis_size(a) for a in ("body", "gx", "gy"))
    _, comp, cx, cy, nz = disp.shape
    bpd, sblk, _ = mortar.shape
    f32 = jnp.float32
    any_spec = pl.BlockSpec(memory_space=pl.ANY)
    vmem = pl.BlockSpec(memory_space=pltpu.VMEM)
    rows = cy + 2 * YB
    dma = pltpu.SemaphoreType.DMA
    return pl.pallas_call(
        functools.partial(kernel, nb, ngx, ngy),
        out_shape=(jax.ShapeDtypeStruct(disp.shape, f32), jax.ShapeDtypeStruct(gap0.shape, f32)),
        in_specs=[any_spec] * 9,
        out_specs=(vmem, vmem),
        scratch_shapes=[
            pltpu.VMEM((bpd, sblk), f32),
            pltpu.VMEM((bpd, sblk), f32),
            pltpu.SMEM((bpd,), jnp.int32),
            pltpu.SMEM((bpd,), jnp.int32),
            pltpu.VMEM((comp + 1, cx + 2, rows, nz), f32),
            pltpu.VMEM((comp, cx + 2, rows, nz), f32),
            pltpu.VMEM((comp, cx + 2, rows, nz), f32),
            pltpu.VMEM((comp, cx, cy, nz), f32),
            pltpu.VMEM((cx, cy, nz), f32),
            pltpu.VMEM((comp, cx, cy, nz), f32),
            pltpu.VMEM((cx, cy, nz), f32),
            pltpu.VMEM((bpd, sblk, sblk), f32),
            pltpu.VMEM((3, nb, ngx, bpd + 2, sblk), f32),
            pltpu.VMEM((3, ngx, bpd, sblk), f32),
            pltpu.VMEM((3, ngx, bpd, sblk), f32),
            pltpu.VMEM((1, ngy, 2, sblk), f32),
            pltpu.VMEM((nb * ngx * ngy, 2, sblk), f32),
            pltpu.VMEM((7, bpd, sblk, 1), f32),
            dma((9,)),
            dma((3, len(DIRS))), dma((3, len(DIRS))),
            dma((3, nb * ngx)), dma((3, nb * ngx)),
            dma((3, ngx)), dma((3, ngx)),
            dma((1, ngy)), dma((1, ngy)),
            dma((nb * ngx * ngy,)), dma((nb * ngx * ngy,)),
        ],
        compiler_params=pltpu.CompilerParams(collective_id=0, has_side_effects=True,
                                             vmem_limit_bytes=60 * 1024 * 1024),
        name="newton_step",
    )(disp, force, kappa, sigma, gap0, pressure, mortar, partner, active)


def solution(mesh):
    placed = (
        P("body", None, "gx", "gy", None),
        P("body", None, "gx", "gy", None),
        P("body", "gx", "gy", None),
        P("body", "gx", "gy", None),
        P(("gx", "gy"), None),
        P(("gx", "gy"), None),
        P(("gx", "gy"), None, None),
        P(("gx", "gy")),
        P(("gx", "gy")),
    )
    return jax.shard_map(
        on_device,
        mesh=mesh,
        in_specs=placed,
        out_specs=(P("body", None, "gx", "gy", None), P(("gx", "gy"), None)),
        check_vma=False,
    )
```

```python
import functools

import jax
import jax.numpy as jnp
from jax import lax
from jax.experimental import pallas as pl
from jax.experimental.pallas import tpu as pltpu
from jax.sharding import PartitionSpec as P

MESH = pl.DeviceIdType.MESH
YB = 8
DIRS = tuple((dx, dy) for dx in (-1, 0, 1) for dy in (-1, 0, 1) if dx != 0 or dy != 0)


def kernel(nb, ngx, ngy, disp, force, kappa, sigma, gap0_in, press_in, mortar, partner_in, active_in,
           inc_out, np_out, gap0, press, partner, active, f0, f1, f2, v2, diag, force_v, sigma_v, mort, surf, usend, urecv,
           dots, grecv, final, cols, load_sem, hs, hr, ss, sr, us, ur, ds, dr, gs, gr, fs, fr):
    comp, cx, cy, nz = force_v.shape
    bpd, sblk = gap0.shape
    per = sblk // cy
    b = lax.axis_index("body")
    gx = lax.axis_index("gx")
    gy = lax.axis_index("gy")

    loads = [
        pltpu.make_async_copy(disp.at[0], f0.at[pl.ds(0, comp), pl.ds(1, cx), pl.ds(YB, cy)], load_sem.at[0]),
        pltpu.make_async_copy(kappa.at[0], f0.at[comp, pl.ds(1, cx), pl.ds(YB, cy)], load_sem.at[1]),
        pltpu.make_async_copy(mortar, mort, load_sem.at[2]),
        pltpu.make_async_copy(sigma.at[0], sigma_v, load_sem.at[3]),
        pltpu.make_async_copy(force.at[0], force_v, load_sem.at[4]),
        pltpu.make_async_copy(gap0_in, gap0, load_sem.at[5]),
        pltpu.make_async_copy(press_in, press, load_sem.at[6]),
        pltpu.make_async_copy(partner_in, partner, load_sem.at[7]),
        pltpu.make_async_copy(active_in, active, load_sem.at[8]),
    ]
    for load in loads:
        load.start()

    def exists(dx, dy):
        good = jnp.bool_(True)
        if dx < 0:
            good = good & (gx >= 1)
        if dx > 0:
            good = good & (gx < ngx - 1)
        if dy < 0:
            good = good & (gy >= 1)
        if dy > 0:
            good = good & (gy < ngy - 1)
        return good

    row_peers = [(db, k) for db in range(nb) for k in range(ngx) if db or k]
    barrier = pltpu.get_barrier_semaphore()
    for db, k in row_peers:
        pl.semaphore_signal(barrier, inc=1, device_id={"body": lax.rem(b + db, nb), "gx": lax.rem(gx + k, ngx)},
                            device_id_type=MESH)
    for k in range(1, ngy):
        pl.semaphore_signal(barrier, inc=1, device_id={"gy": lax.rem(gy + k, ngy)}, device_id_type=MESH)
    expect = len(row_peers) + ngy - 1
    for dx, dy in DIRS:
        if dx and dy:
            here = exists(dx, dy)
            expect = expect + here.astype(jnp.int32)

            @pl.when(here)
            def _():
                pl.semaphore_signal(barrier, inc=1, device_id={"gx": gx + dx, "gy": gy + dy}, device_id_type=MESH)

    for side, x in ((-1, 0), (1, cx + 1)):
        @pl.when(jnp.logical_not(exists(side, 0)))
        def _():
            for f in (f0, f1, f2):
                for c in range(f.shape[0]):
                    f[c, x, YB - 1 : YB] = jnp.zeros((1, nz), f.dtype)
                    f[c, x, YB : YB + cy] = jnp.zeros((cy, nz), f.dtype)
                    f[c, x, YB + cy : YB + cy + 1] = jnp.zeros((1, nz), f.dtype)
    for side, y in ((-1, YB - 1), (1, YB + cy)):
        @pl.when(jnp.logical_not(exists(0, side)))
        def _():
            for f in (f0, f1, f2):
                for c in range(f.shape[0]):
                    for x in range(cx + 2):
                        f[c, x, y : y + 1] = jnp.zeros((1, nz), f.dtype)

    lane = lax.broadcasted_iota(jnp.int32, (sblk, nz), 1)
    eye = lax.broadcasted_iota(jnp.int32, (sblk, nz), 0) == lane
    first_lane = lane == 0
    lane_row = lax.broadcasted_iota(jnp.int32, (cy, nz), 1)
    left_w = jnp.where(lane_row == 0, 0.0, 0.5)
    right_w = jnp.where(lane_row == nz - 1, 0.0, 0.5)

    def to_col(row):
        return jnp.sum(jnp.where(eye, row, 0.0), axis=1, keepdims=True)

    def to_row(col):
        return jnp.sum(jnp.where(eye, col, 0.0), axis=0, keepdims=True)

    def tz(v):
        return v + left_w * pltpu.roll(v, 1, 1) + right_w * pltpu.roll(v, nz - 1, 1)

    def surface_rows(f, r):
        for l in range(bpd):
            block = f[comp - 1, 1 + l * per : 1 + (l + 1) * per, YB : YB + cy, :].reshape(sblk, nz)
            surf[r, b, gx, l : l + 1, :] = to_row(block[:, 0:1])

    pending = []

    def halo_copy(f, r, d, dx, dy, sending):
        def part(delta, size, base):
            if delta == 0:
                return pl.ds(base, size), pl.ds(base, size)
            if delta < 0:
                return pl.ds(base, 1), pl.ds(base + size, 1)
            return pl.ds(base + size - 1, 1), pl.ds(base - 1, 1)
        sx, tx = part(dx, cx, 1)
        sy, ty = part(dy, cy, YB)
        allc = pl.ds(0, f.shape[0])
        return pltpu.make_async_remote_copy(
            src_ref=f.at[allc, sx, sy], dst_ref=f.at[allc, tx, ty], send_sem=hs.at[r, d], recv_sem=hr.at[r, d],
            device_id={"gx": gx + dx, "gy": gy + dy}, device_id_type=MESH)

    def halo_send(f, r):
        for d, (dx, dy) in enumerate(DIRS):
            @pl.when(exists(dx, dy))
            def _():
                halo_copy(f, r, d, dx, dy, True).start()

    def halo_wait(f, r):
        for d, (dx, dy) in enumerate(DIRS):
            @pl.when(exists(-dx, -dy))
            def _():
                halo_copy(f, r, d, dx, dy, False).wait_recv()

    def halo_done(f, r):
        for d, (dx, dy) in enumerate(DIRS):
            @pl.when(exists(dx, dy))
            def _():
                halo_copy(f, r, d, dx, dy, True).wait_send()

    def surf_copy(r, i, db, k, incoming):
        ob, og = lax.rem(b + db, nb), lax.rem(gx + k, ngx)
        wb, wg = (ob, og) if incoming else (b, gx)
        return pltpu.make_async_remote_copy(
            src_ref=surf.at[r, wb, wg], dst_ref=surf.at[r, wb, wg], send_sem=ss.at[r, i],
            recv_sem=sr.at[r, wb * ngx + wg], device_id={"body": ob, "gx": og}, device_id_type=MESH)

    def surf_each(r, incoming, act):
        for i, (db, k) in enumerate(row_peers):
            def go():
                act(surf_copy(r, i, db, k, incoming))
            if db == 1 and k == 0:
                go()
            else:
                origin = lax.rem(b + db, nb) if incoming else b
                pl.when(origin == 1)(go)

    def surf_send(r):
        surf_each(r, False, lambda copy: copy.start())

    def surf_wait(r):
        surf_each(r, True, lambda copy: copy.wait_recv())

    def u_copy(r, k, incoming):
        og = lax.rem(gx + k, ngx)
        return pltpu.make_async_remote_copy(
            src_ref=usend.at[r, og], dst_ref=urecv.at[r, og if incoming else gx], send_sem=us.at[r, k],
            recv_sem=ur.at[r, og if incoming else gx], device_id={"gx": og}, device_id_type=MESH)

    def g_copy(s, k, incoming):
        og = lax.rem(gy + k, ngy)
        w = og if incoming else gy
        return pltpu.make_async_remote_copy(
            src_ref=grecv.at[s, w], dst_ref=grecv.at[s, w], send_sem=gs.at[s, k], recv_sem=gr.at[s, w],
            device_id={"gy": og}, device_id_type=MESH)

    def scalars(total):
        return (jnp.sum(total[0:1, :], axis=1, keepdims=True), jnp.sum(total[1:2, :], axis=1, keepdims=True))

    def dot_copy(i, db, k, incoming):
        ob, og = lax.rem(b + db, nb), lax.rem(gx + k, ngx)
        wb, wg = (ob, og) if incoming else (b, gx)
        return pltpu.make_async_remote_copy(
            src_ref=dots.at[wb, wg], dst_ref=dots.at[wb, wg], send_sem=ds.at[i],
            recv_sem=dr.at[wb * ngx + wg], device_id={"body": ob, "gx": og}, device_id_type=MESH)

    def g_send():
        for i, (db, k) in enumerate(row_peers):
            dot_copy(i, db, k, True).wait_recv()
        total = dots[0, 0]
        for w in range(1, nb * ngx):
            total = total + dots[w // ngx, w % ngx]
        grecv[0, gy] = total
        for k in range(1, ngy):
            g_copy(0, k, False).start()

    def g_take():
        for k in range(1, ngy):
            g_copy(0, k, True).wait_recv()
        total = grecv[0, 0]
        for w in range(1, ngy):
            total = total + grecv[0, w]
        return scalars(total)

    count = nb * ngx * ngy
    me = (b * ngx + gx) * ngy + gy

    def each_peer(act):
        if count <= 64:
            for k in range(1, count):
                act(k)
        else:
            pl.loop(1, count)(act)

    def final_copy(k, incoming):
        other = lax.rem(me + k, count)
        w = other if incoming else me
        return pltpu.make_async_remote_copy(
            src_ref=final.at[w], dst_ref=final.at[w], send_sem=fs.at[k], recv_sem=fr.at[w],
            device_id={"body": other // (ngx * ngy), "gx": lax.rem(other // ngy, ngx), "gy": lax.rem(other, ngy)},
            device_id_type=MESH)

    def b_of(r, l):
        picked = jnp.zeros((1, sblk), jnp.float32)
        for g in range(ngx):
            for q in range(bpd):
                picked = picked + jnp.where(partner[l] == g * bpd + q, surf[r, 1, g, q : q + 1, :], 0.0)
        slave = surf[r, 0, gx, l : l + 1, :]
        return -jnp.sum(mort[l] * picked + jnp.where(eye, slave, 0.0), axis=1, keepdims=True)

    def u_start(r):
        pulled = [jnp.sum(mort[l] * cols[5, l], axis=0, keepdims=True) for l in range(bpd)]
        for g in range(ngx):
            for q in range(bpd):
                row = jnp.zeros((1, sblk), jnp.float32)
                for l in range(bpd):
                    row = row + jnp.where(partner[l] == g * bpd + q, pulled[l], 0.0)
                usend[r, g, q : q + 1, :] = row

        @pl.when(b == 1)
        def _():
            for k in range(1, ngx):
                u_copy(r, k, False).start()

    def u_finish(r, f):
        def add(l, col):
            xs = slice(1 + l * per, 1 + (l + 1) * per)
            block = f[comp - 1, xs, YB : YB + cy, :].reshape(sblk, nz)
            f[comp - 1, xs, YB : YB + cy, :] = (block - jnp.where(first_lane, col, 0.0)).reshape(per, cy, nz)

        @pl.when(b == 0)
        def _():
            for l in range(bpd):
                add(l, cols[5, l])

        @pl.when(b == 1)
        def _():
            for k in range(1, ngx):
                u_copy(r, k, True).wait_recv()
            urecv[r, gx] = usend[r, gx]
            for l in range(bpd):
                row = urecv[r, 0, l : l + 1, :]
                for g in range(1, ngx):
                    row = row + urecv[r, g, l : l + 1, :]
                add(l, to_col(row))

    def apply(f, emit):
        @pl.loop(0, comp)
        def _(c):
            window = []
            for x in range(cx + 2):
                kap = [f0[comp, x, YB + s : YB + s + cy, :] for s in (-1, 0, 1)]
                val = [f[c, x, YB + s : YB + s + cy, :] for s in (-1, 0, 1)]
                window.append((val[1] + 0.5 * (val[0] + val[2]),
                               kap[1] * val[1] + 0.5 * (kap[0] * val[0] + kap[2] * val[2])))
                if x >= 2:
                    p = window[x - 1][0] + 0.5 * (window[x - 2][0] + window[x][0])
                    q = window[x - 1][1] + 0.5 * (window[x - 2][1] + window[x][1])
                    k0 = f0[comp, x - 1, YB : YB + cy, :]
                    v0 = f[c, x - 1, YB : YB + cy, :]
                    emit(c, x - 2, diag[x - 2] * v0 - k0 * tz(p) - tz(q))

    loads[0].wait()
    loads[1].wait()
    surface_rows(f0, 0)
    pl.semaphore_wait(barrier, expect)

    surf_send(0)
    halo_send(f0, 0)
    for load in loads[2:]:
        load.wait()
    surf_wait(0)
    for l in range(bpd):
        gap = to_col(gap0[l : l + 1, :]) + b_of(0, l)
        prs = to_col(press[l : l + 1, :])
        radius = jnp.sqrt(gap * gap + prs * prs + 0.01)
        complement = gap + prs - radius
        slope_gap = 1.0 - gap / radius
        divisor = (1.0 - prs / radius) + 0.5
        flag = active[l].astype(jnp.float32)
        cols[0, l] = flag * slope_gap / divisor
        cols[1, l] = complement / divisor
        cols[2, l] = slope_gap / divisor
        cols[5, l] = flag * prs - flag * complement / divisor
    u_start(0)
    halo_wait(f0, 0)
    window = []
    for x in range(cx + 2):
        kap = [f0[comp, x, YB + s : YB + s + cy, :] for s in (-1, 0, 1)]
        window.append(kap[1] + 0.5 * (kap[0] + kap[2]))
        if x >= 2:
            p = window[x - 1] + 0.5 * (window[x - 2] + window[x])
            diag[x - 2] = sigma_v[x - 2] + 8.0 * f0[comp, x - 1, YB : YB + cy, :] + tz(p)

    def emit_rhs(c, x, val):
        f1[c, 1 + x, YB : YB + cy, :] = force_v[c, x] - val

    apply(f0, emit_rhs)
    u_finish(0, f1)

    surface_rows(f1, 1)
    surf_send(1)
    halo_send(f1, 1)
    surf_wait(1)
    for l in range(bpd):
        gap = b_of(1, l)
        cols[3, l] = gap
        cols[5, l] = cols[0, l] * gap
    u_start(1)
    halo_wait(f1, 1)

    def emit_v1(c, x, val):
        f2[c, 1 + x, YB : YB + cy, :] = val

    apply(f1, emit_v1)

    def sum_of(left, right):
        total = jnp.zeros((cy, nz), jnp.float32)
        for c in range(comp):
            for x in range(cx):
                total = total + left(c, x) * right(c, x)
        return jnp.sum(total, axis=0, keepdims=True)

    first_row = lax.broadcasted_iota(jnp.int32, (1, nz), 1) == 0
    slave_side = (b == 0).astype(jnp.float32)

    def contact_sum(left, right):
        total = jnp.zeros((1, 1), jnp.float32)
        for l in range(bpd):
            total = total + jnp.sum(cols[0, l] * left(l) * right(l), axis=0, keepdims=True)
        return jnp.where(first_row, slave_side * total, 0.0)

    def r0_of(c, x):
        return f1[c, 1 + x, YB : YB + cy, :]

    def v1_of(c, x):
        return f2[c, 1 + x, YB : YB + cy, :]

    dots[b, gx, 0:1, :] = sum_of(r0_of, r0_of)
    dots[b, gx, 1:2, :] = sum_of(r0_of, v1_of) + contact_sum(lambda l: cols[3, l], lambda l: cols[3, l])
    for i, (db, k) in enumerate(row_peers):
        dot_copy(i, db, k, False).start()
    u_finish(1, f2)

    surface_rows(f2, 2)
    surf_send(2)
    halo_send(f2, 2)
    g_send()
    surf_wait(2)
    for l in range(bpd):
        cols[4, l] = b_of(2, l)
    halo_wait(f2, 2)

    def emit_v2(c, x, val):
        v2[c, x] = val

    apply(f2, emit_v2)
    norm0, product0 = g_take()
    alpha0 = norm0 / product0

    def r1_of(c, x):
        return r0_of(c, x) - alpha0 * v1_of(c, x)

    norm = sum_of(r1_of, r1_of)
    product = sum_of(r1_of, lambda c, x: v1_of(c, x) - alpha0 * v2[c, x])
    product = product - alpha0 * contact_sum(lambda l: cols[3, l] - alpha0 * cols[4, l], lambda l: cols[4, l])
    final[me, 0:1, :] = norm
    final[me, 1:2, :] = product
    each_peer(lambda k: final_copy(k, False).start())
    each_peer(lambda k: final_copy(k, True).wait_recv())
    norm1, product1 = scalars(lax.fori_loop(1, count, lambda w, t: t + final[w], final[0], unroll=count <= 64))
    ratio = norm1 / norm0
    alpha1 = norm1 / (product1 - ratio * norm1 / alpha0)
    coef_r = alpha0 + alpha1 * (1.0 + ratio)
    coef_v = -alpha1 * alpha0
    for c in range(comp):
        for x in range(cx):
            inc_out[0, c, x] = coef_r * r0_of(c, x) + coef_v * v1_of(c, x)
    for l in range(bpd):
        change = coef_r * cols[3, l] + coef_v * cols[4, l]
        flag = active[l].astype(jnp.float32)
        step = to_row(cols[1, l] + cols[2, l] * change)
        np_out[l : l + 1, :] = flag * (press[l : l + 1, :] - step)

    for r, f in enumerate((f0, f1, f2)):
        halo_done(f, r)
    for r in range(3):
        surf_each(r, False, lambda copy: copy.wait_send())
    for i, (db, k) in enumerate(row_peers):
        dot_copy(i, db, k, False).wait_send()
    for k in range(1, ngy):
        g_copy(0, k, False).wait_send()
    each_peer(lambda k: final_copy(k, False).wait_send())

    @pl.when(b == 1)
    def _():
        for r in range(2):
            for k in range(1, ngx):
                u_copy(r, k, False).wait_send()


def on_device(disp, force, kappa, sigma, gap0, pressure, mortar, partner, active):
    nb, ngx, ngy = (lax.axis_size(a) for a in ("body", "gx", "gy"))
    _, comp, cx, cy, nz = disp.shape
    bpd, sblk, _ = mortar.shape
    f32 = jnp.float32
    any_spec = pl.BlockSpec(memory_space=pl.ANY)
    vmem = pl.BlockSpec(memory_space=pltpu.VMEM)
    rows = cy + 2 * YB
    dma = pltpu.SemaphoreType.DMA
    return pl.pallas_call(
        functools.partial(kernel, nb, ngx, ngy),
        out_shape=(pltpu.VMEM(disp.shape, f32), pltpu.VMEM(gap0.shape, f32)),
        in_specs=[any_spec] * 9,
        out_specs=(vmem, vmem),
        scratch_shapes=[
            pltpu.VMEM((bpd, sblk), f32),
            pltpu.VMEM((bpd, sblk), f32),
            pltpu.SMEM((bpd,), jnp.int32),
            pltpu.SMEM((bpd,), jnp.int32),
            pltpu.VMEM((comp + 1, cx + 2, rows, nz), f32),
            pltpu.VMEM((comp, cx + 2, rows, nz), f32),
            pltpu.VMEM((comp, cx + 2, rows, nz), f32),
            pltpu.VMEM((comp, cx, cy, nz), f32),
            pltpu.VMEM((cx, cy, nz), f32),
            pltpu.VMEM((comp, cx, cy, nz), f32),
            pltpu.VMEM((cx, cy, nz), f32),
            pltpu.VMEM((bpd, sblk, sblk), f32),
            pltpu.VMEM((3, nb, ngx, bpd, sblk), f32),
            pltpu.VMEM((2, ngx, bpd, sblk), f32),
            pltpu.VMEM((2, ngx, bpd, sblk), f32),
            pltpu.VMEM((nb, ngx, 2, sblk), f32),
            pltpu.VMEM((1, ngy, 2, sblk), f32),
            pltpu.VMEM((nb * ngx * ngy, 2, sblk), f32),
            pltpu.VMEM((6, bpd, sblk, 1), f32),
            dma((9,)),
            dma((3, len(DIRS))), dma((3, len(DIRS))),
            dma((3, nb * ngx)), dma((3, nb * ngx)),
            dma((2, ngx)), dma((2, ngx)),
            dma((nb * ngx,)), dma((nb * ngx,)),
            dma((1, ngy)), dma((1, ngy)),
            dma((nb * ngx * ngy,)), dma((nb * ngx * ngy,)),
        ],
        compiler_params=pltpu.CompilerParams(collective_id=0, has_side_effects=True,
                                             vmem_limit_bytes=60 * 1024 * 1024),
        name="newton_step",
    )(disp, force, kappa, sigma, gap0, pressure, mortar, partner, active)


def solution(mesh):
    placed = (
        P("body", None, "gx", "gy", None),
        P("body", None, "gx", "gy", None),
        P("body", "gx", "gy", None),
        P("body", "gx", "gy", None),
        P(("gx", "gy"), None),
        P(("gx", "gy"), None),
        P(("gx", "gy"), None, None),
        P(("gx", "gy")),
        P(("gx", "gy")),
    )
    return jax.shard_map(
        on_device,
        mesh=mesh,
        in_specs=placed,
        out_specs=(P("body", None, "gx", "gy", None), P(("gx", "gy"), None)),
        check_vma=False,
    )
```

```python
import functools

import jax
import jax.numpy as jnp
from jax import lax
from jax.experimental import pallas as pl
from jax.experimental.pallas import tpu as pltpu
from jax.sharding import PartitionSpec as P

MESH = pl.DeviceIdType.MESH
YB = 8
DIRS = tuple((dx, dy) for dx in (-1, 0, 1) for dy in (-1, 0, 1) if dx != 0 or dy != 0)


def kernel(nb, ngx, ngy, disp, force, kappa, sigma, gap0_in, press_in, mortar, partner_in, active_in,
           inc_out, np_out, gap0, press, partner, active, f0, f1, f2, v2, diag, force_v, sigma_v, mort, surf, usend, urecv,
           final, cols, load_sem, hs, hr, ss, sr, us, ur, fs, fr):
    comp, cx, cy, nz = force_v.shape
    bpd, sblk = gap0.shape
    per = sblk // cy
    b = lax.axis_index("body")
    gx = lax.axis_index("gx")
    gy = lax.axis_index("gy")

    loads = [
        pltpu.make_async_copy(disp.at[0], f0.at[pl.ds(0, comp), pl.ds(1, cx), pl.ds(YB, cy)], load_sem.at[0]),
        pltpu.make_async_copy(kappa.at[0], f0.at[comp, pl.ds(1, cx), pl.ds(YB, cy)], load_sem.at[1]),
        pltpu.make_async_copy(mortar, mort, load_sem.at[2]),
        pltpu.make_async_copy(sigma.at[0], sigma_v, load_sem.at[3]),
        pltpu.make_async_copy(force.at[0], force_v, load_sem.at[4]),
        pltpu.make_async_copy(gap0_in, gap0, load_sem.at[5]),
        pltpu.make_async_copy(press_in, press, load_sem.at[6]),
        pltpu.make_async_copy(partner_in, partner, load_sem.at[7]),
        pltpu.make_async_copy(active_in, active, load_sem.at[8]),
    ]
    for load in loads:
        load.start()

    def exists(dx, dy):
        good = jnp.bool_(True)
        if dx < 0:
            good = good & (gx >= 1)
        if dx > 0:
            good = good & (gx < ngx - 1)
        if dy < 0:
            good = good & (gy >= 1)
        if dy > 0:
            good = good & (gy < ngy - 1)
        return good

    row_peers = [(db, k) for db in range(nb) for k in range(ngx) if db or k]
    count = nb * ngx * ngy
    me = (b * ngx + gx) * ngy + gy

    def place_of(other):
        return {"body": other // (ngx * ngy), "gx": lax.rem(other // ngy, ngx), "gy": lax.rem(other, ngy)}

    def each_peer(act):
        if count <= 64:
            for k in range(1, count):
                act(k)
        else:
            pl.loop(1, count)(act)

    barrier = pltpu.get_barrier_semaphore()
    if ngy <= 4:
        for db, k in row_peers:
            pl.semaphore_signal(barrier, inc=1, device_id={"body": lax.rem(b + db, nb), "gx": lax.rem(gx + k, ngx)},
                                device_id_type=MESH)
        expect = len(row_peers)
        for dx, dy in DIRS:
            if dy:
                here = exists(dx, dy)
                expect = expect + here.astype(jnp.int32)

                @pl.when(here)
                def _():
                    pl.semaphore_signal(barrier, inc=1, device_id={"gx": gx + dx, "gy": gy + dy}, device_id_type=MESH)
    else:
        each_peer(lambda k: pl.semaphore_signal(barrier, inc=1, device_id=place_of(lax.rem(me + k, count)),
                                                device_id_type=MESH))
        expect = count - 1

    for side, x in ((-1, 0), (1, cx + 1)):
        @pl.when(jnp.logical_not(exists(side, 0)))
        def _():
            for f in (f0, f1, f2):
                for c in range(f.shape[0]):
                    f[c, x, YB - 1 : YB] = jnp.zeros((1, nz), f.dtype)
                    f[c, x, YB : YB + cy] = jnp.zeros((cy, nz), f.dtype)
                    f[c, x, YB + cy : YB + cy + 1] = jnp.zeros((1, nz), f.dtype)
    for side, y in ((-1, YB - 1), (1, YB + cy)):
        @pl.when(jnp.logical_not(exists(0, side)))
        def _():
            for f in (f0, f1, f2):
                for c in range(f.shape[0]):
                    for x in range(cx + 2):
                        f[c, x, y : y + 1] = jnp.zeros((1, nz), f.dtype)

    lane = lax.broadcasted_iota(jnp.int32, (sblk, nz), 1)
    eye = lax.broadcasted_iota(jnp.int32, (sblk, nz), 0) == lane
    first_lane = lane == 0
    lane_row = lax.broadcasted_iota(jnp.int32, (cy, nz), 1)
    left_w = jnp.where(lane_row == 0, 0.0, 0.5)
    right_w = jnp.where(lane_row == nz - 1, 0.0, 0.5)

    def to_col(row):
        return jnp.sum(jnp.where(eye, row, 0.0), axis=1, keepdims=True)

    def to_row(col):
        return jnp.sum(jnp.where(eye, col, 0.0), axis=0, keepdims=True)

    def tz(v):
        return v + left_w * pltpu.roll(v, 1, 1) + right_w * pltpu.roll(v, nz - 1, 1)

    def surface_rows(f, r):
        for l in range(bpd):
            block = f[comp - 1, 1 + l * per : 1 + (l + 1) * per, YB : YB + cy, :].reshape(sblk, nz)
            surf[r, b, gx, l : l + 1, :] = to_row(block[:, 0:1])

    pending = []

    def halo_copy(f, r, d, dx, dy, sending):
        def part(delta, size, base):
            if delta == 0:
                return pl.ds(base, size), pl.ds(base, size)
            if delta < 0:
                return pl.ds(base, 1), pl.ds(base + size, 1)
            return pl.ds(base + size - 1, 1), pl.ds(base - 1, 1)
        sx, tx = part(dx, cx, 1)
        sy, ty = part(dy, cy, YB)
        allc = pl.ds(0, f.shape[0])
        return pltpu.make_async_remote_copy(
            src_ref=f.at[allc, sx, sy], dst_ref=f.at[allc, tx, ty], send_sem=hs.at[r, d], recv_sem=hr.at[r, d],
            device_id={"gx": gx + dx, "gy": gy + dy}, device_id_type=MESH)

    def halo_send(f, r):
        for d, (dx, dy) in enumerate(DIRS):
            @pl.when(exists(dx, dy))
            def _():
                halo_copy(f, r, d, dx, dy, True).start()

    def halo_wait(f, r):
        for d, (dx, dy) in enumerate(DIRS):
            @pl.when(exists(-dx, -dy))
            def _():
                halo_copy(f, r, d, dx, dy, False).wait_recv()

    def halo_done(f, r):
        for d, (dx, dy) in enumerate(DIRS):
            @pl.when(exists(dx, dy))
            def _():
                halo_copy(f, r, d, dx, dy, True).wait_send()

    def surf_copy(r, i, db, k, incoming):
        ob, og = lax.rem(b + db, nb), lax.rem(gx + k, ngx)
        wb, wg = (ob, og) if incoming else (b, gx)
        return pltpu.make_async_remote_copy(
            src_ref=surf.at[r, wb, wg], dst_ref=surf.at[r, wb, wg], send_sem=ss.at[r, i],
            recv_sem=sr.at[r, wb * ngx + wg], device_id={"body": ob, "gx": og}, device_id_type=MESH)

    def surf_each(r, incoming, act):
        for i, (db, k) in enumerate(row_peers):
            def go():
                act(surf_copy(r, i, db, k, incoming))
            if db == 1 and k == 0:
                go()
            else:
                origin = lax.rem(b + db, nb) if incoming else b
                pl.when(origin == 1)(go)

    def surf_send(r):
        surf_each(r, False, lambda copy: copy.start())

    def surf_wait(r):
        surf_each(r, True, lambda copy: copy.wait_recv())

    def u_copy(r, k, incoming):
        og = lax.rem(gx + k, ngx)
        return pltpu.make_async_remote_copy(
            src_ref=usend.at[r, og], dst_ref=urecv.at[r, og if incoming else gx], send_sem=us.at[r, k],
            recv_sem=ur.at[r, og if incoming else gx], device_id={"gx": og}, device_id_type=MESH)

    def final_copy(k, incoming):
        other = lax.rem(me + k, count)
        w = other if incoming else me
        return pltpu.make_async_remote_copy(
            src_ref=final.at[w], dst_ref=final.at[w], send_sem=fs.at[k], recv_sem=fr.at[w],
            device_id=place_of(other),
            device_id_type=MESH)

    def b_of(r, l):
        picked = jnp.zeros((1, sblk), jnp.float32)
        for g in range(ngx):
            for q in range(bpd):
                picked = picked + jnp.where(partner[l] == g * bpd + q, surf[r, 1, g, q : q + 1, :], 0.0)
        slave = surf[r, 0, gx, l : l + 1, :]
        return -jnp.sum(mort[l] * picked + jnp.where(eye, slave, 0.0), axis=1, keepdims=True)

    def u_start(r):
        pulled = [jnp.sum(mort[l] * cols[5, l], axis=0, keepdims=True) for l in range(bpd)]
        for g in range(ngx):
            for q in range(bpd):
                row = jnp.zeros((1, sblk), jnp.float32)
                for l in range(bpd):
                    row = row + jnp.where(partner[l] == g * bpd + q, pulled[l], 0.0)
                usend[r, g, q : q + 1, :] = row

        @pl.when(b == 1)
        def _():
            for k in range(1, ngx):
                u_copy(r, k, False).start()

    def u_finish(r, f):
        def add(l, col):
            xs = slice(1 + l * per, 1 + (l + 1) * per)
            block = f[comp - 1, xs, YB : YB + cy, :].reshape(sblk, nz)
            f[comp - 1, xs, YB : YB + cy, :] = (block - jnp.where(first_lane, col, 0.0)).reshape(per, cy, nz)

        @pl.when(b == 0)
        def _():
            for l in range(bpd):
                add(l, cols[5, l])

        @pl.when(b == 1)
        def _():
            for k in range(1, ngx):
                u_copy(r, k, True).wait_recv()
            urecv[r, gx] = usend[r, gx]
            for l in range(bpd):
                row = urecv[r, 0, l : l + 1, :]
                for g in range(1, ngx):
                    row = row + urecv[r, g, l : l + 1, :]
                add(l, to_col(row))

    def apply(f, emit):
        @pl.loop(0, comp)
        def _(c):
            window = []
            for x in range(cx + 2):
                kap = [f0[comp, x, YB + s : YB + s + cy, :] for s in (-1, 0, 1)]
                val = [f[c, x, YB + s : YB + s + cy, :] for s in (-1, 0, 1)]
                window.append((val[1] + 0.5 * (val[0] + val[2]),
                               kap[1] * val[1] + 0.5 * (kap[0] * val[0] + kap[2] * val[2])))
                if x >= 2:
                    p = window[x - 1][0] + 0.5 * (window[x - 2][0] + window[x][0])
                    q = window[x - 1][1] + 0.5 * (window[x - 2][1] + window[x][1])
                    k0 = f0[comp, x - 1, YB : YB + cy, :]
                    v0 = f[c, x - 1, YB : YB + cy, :]
                    emit(c, x - 2, diag[x - 2] * v0 - k0 * tz(p) - tz(q))

    loads[0].wait()
    loads[1].wait()
    surface_rows(f0, 0)
    pl.semaphore_wait(barrier, expect)

    surf_send(0)
    halo_send(f0, 0)
    for load in loads[2:]:
        load.wait()
    surf_wait(0)
    for l in range(bpd):
        gap = to_col(gap0[l : l + 1, :]) + b_of(0, l)
        prs = to_col(press[l : l + 1, :])
        radius = jnp.sqrt(gap * gap + prs * prs + 0.01)
        per_radius = 1.0 / radius
        complement = gap + prs - radius
        per_divisor = 1.0 / ((1.0 - prs * per_radius) + 0.5)
        flag = active[l].astype(jnp.float32)
        cols[1, l] = complement * per_divisor
        cols[2, l] = (1.0 - gap * per_radius) * per_divisor
        cols[5, l] = flag * (prs - complement * per_divisor)
    u_start(0)
    for l in range(bpd):
        cols[0, l] = active[l].astype(jnp.float32) * cols[2, l]
    halo_wait(f0, 0)
    window = []
    for x in range(cx + 2):
        kap = [f0[comp, x, YB + s : YB + s + cy, :] for s in (-1, 0, 1)]
        window.append(kap[1] + 0.5 * (kap[0] + kap[2]))
        if x >= 2:
            p = window[x - 1] + 0.5 * (window[x - 2] + window[x])
            diag[x - 2] = sigma_v[x - 2] + 8.0 * f0[comp, x - 1, YB : YB + cy, :] + tz(p)

    def emit_rhs(c, x, val):
        f1[c, 1 + x, YB : YB + cy, :] = force_v[c, x] - val

    apply(f0, emit_rhs)
    u_finish(0, f1)

    surface_rows(f1, 1)
    surf_send(1)
    halo_send(f1, 1)
    surf_wait(1)
    for l in range(bpd):
        gap = b_of(1, l)
        cols[3, l] = gap
        cols[5, l] = cols[0, l] * gap
    u_start(1)
    halo_wait(f1, 1)

    def emit_v1(c, x, val):
        f2[c, 1 + x, YB : YB + cy, :] = val

    apply(f1, emit_v1)

    def sum_of(left, right):
        total = jnp.zeros((cy, nz), jnp.float32)
        for c in range(comp):
            for x in range(cx):
                total = total + left(c, x) * right(c, x)
        return jnp.sum(jnp.sum(total, axis=0, keepdims=True), axis=1, keepdims=True)

    slave_side = (b == 0).astype(jnp.float32)

    def contact_sum(left, right):
        total = jnp.zeros((1, 1), jnp.float32)
        for l in range(bpd):
            total = total + jnp.sum(cols[0, l] * left(l) * right(l), axis=0, keepdims=True)
        return slave_side * total

    def r0_of(c, x):
        return f1[c, 1 + x, YB : YB + cy, :]

    def v1_of(c, x):
        return f2[c, 1 + x, YB : YB + cy, :]

    u_finish(1, f2)

    surface_rows(f2, 2)
    surf_send(2)
    halo_send(f2, 2)
    rr = sum_of(r0_of, r0_of)
    rv = sum_of(r0_of, v1_of)
    vv = sum_of(v1_of, v1_of)
    own = jnp.where(vv > 0.0, rv / jnp.where(vv > 0.0, vv, 1.0), 0.0)

    def near_of(c, x):
        return r0_of(c, x) - own * v1_of(c, x)

    nn = sum_of(near_of, near_of)
    nv = sum_of(near_of, v1_of)
    surf_wait(2)
    for l in range(bpd):
        cols[4, l] = b_of(2, l)
    halo_wait(f2, 2)

    def emit_v2(c, x, val):
        v2[c, x] = val

    apply(f2, emit_v2)
    nw = sum_of(near_of, lambda c, x: v2[c, x]) + contact_sum(lambda l: cols[3, l] - own * cols[4, l], lambda l: cols[4, l])
    vw = sum_of(v1_of, lambda c, x: v2[c, x]) + contact_sum(lambda l: cols[4, l], lambda l: cols[4, l])

    lane_of = lax.broadcasted_iota(jnp.int32, (1, sblk), 1)
    for i, number in enumerate((rr, rv, vv, nn, nv, nw, vw, own)):
        final[me, i : i + 1, :] = jnp.where(lane_of == lax.rem(me, sblk), number, 0.0)
    each_peer(lambda k: final_copy(k, False).start())
    for r, f in enumerate((f0, f1, f2)):
        halo_done(f, r)
    for r in range(3):
        surf_each(r, False, lambda copy: copy.wait_send())
    @pl.when(b == 1)
    def _():
        for r in range(2):
            for k in range(1, ngx):
                u_copy(r, k, False).wait_send()

    each_peer(lambda k: final_copy(k, True).wait_recv())
    groups = []
    for start in range(0, count, sblk):
        stop = min(start + sblk, count)
        groups.append(lax.fori_loop(start + 1, stop, lambda w, t: t + final[w], final[start], unroll=count <= 64))

    def over(act):
        total = act(*[groups[0][i : i + 1, :] for i in range(8)])
        for group in groups[1:]:
            total = total + act(*[group[i : i + 1, :] for i in range(8)])
        return jnp.sum(total, axis=1, keepdims=True)

    norm0 = over(lambda rr, rv, vv, nn, nv, nw, vw, own: rr)
    alpha0 = norm0 / over(lambda rr, rv, vv, nn, nv, nw, vw, own: rv)
    norm1 = over(lambda rr, rv, vv, nn, nv, nw, vw, own: nn - (alpha0 - own) * (2.0 * nv - (alpha0 - own) * vv))
    product1 = over(lambda rr, rv, vv, nn, nv, nw, vw, own:
                    nv - (alpha0 - own) * vv - alpha0 * (nw - (alpha0 - own) * vw))
    ratio = norm1 / norm0
    alpha1 = norm1 / (product1 - ratio * norm1 / alpha0)
    coef_r = alpha0 + alpha1 * (1.0 + ratio)
    coef_v = -alpha1 * alpha0
    for c in range(comp):
        for x in range(cx):
            inc_out[0, c, x] = coef_r * r0_of(c, x) + coef_v * v1_of(c, x)
    for l in range(bpd):
        change = coef_r * cols[3, l] + coef_v * cols[4, l]
        flag = active[l].astype(jnp.float32)
        step = to_row(cols[1, l] + cols[2, l] * change)
        np_out[l : l + 1, :] = flag * (press[l : l + 1, :] - step)
    each_peer(lambda k: final_copy(k, False).wait_send())


def on_device(disp, force, kappa, sigma, gap0, pressure, mortar, partner, active):
    nb, ngx, ngy = (lax.axis_size(a) for a in ("body", "gx", "gy"))
    _, comp, cx, cy, nz = disp.shape
    bpd, sblk, _ = mortar.shape
    f32 = jnp.float32
    any_spec = pl.BlockSpec(memory_space=pl.ANY)
    vmem = pl.BlockSpec(memory_space=pltpu.VMEM)
    rows = cy + 2 * YB
    dma = pltpu.SemaphoreType.DMA
    return pl.pallas_call(
        functools.partial(kernel, nb, ngx, ngy),
        out_shape=(pltpu.VMEM(disp.shape, f32), pltpu.VMEM(gap0.shape, f32)),
        in_specs=[any_spec] * 9,
        out_specs=(vmem, vmem),
        scratch_shapes=[
            pltpu.VMEM((bpd, sblk), f32),
            pltpu.VMEM((bpd, sblk), f32),
            pltpu.SMEM((bpd,), jnp.int32),
            pltpu.SMEM((bpd,), jnp.int32),
            pltpu.VMEM((comp + 1, cx + 2, rows, nz), f32),
            pltpu.VMEM((comp, cx + 2, rows, nz), f32),
            pltpu.VMEM((comp, cx + 2, rows, nz), f32),
            pltpu.VMEM((comp, cx, cy, nz), f32),
            pltpu.VMEM((cx, cy, nz), f32),
            pltpu.VMEM((comp, cx, cy, nz), f32),
            pltpu.VMEM((cx, cy, nz), f32),
            pltpu.VMEM((bpd, sblk, sblk), f32),
            pltpu.VMEM((3, nb, ngx, bpd, sblk), f32),
            pltpu.VMEM((2, ngx, bpd, sblk), f32),
            pltpu.VMEM((2, ngx, bpd, sblk), f32),
            pltpu.VMEM((nb * ngx * ngy, 8, sblk), f32),
            pltpu.VMEM((6, bpd, sblk, 1), f32),
            dma((9,)),
            dma((3, len(DIRS))), dma((3, len(DIRS))),
            dma((3, nb * ngx)), dma((3, nb * ngx)),
            dma((2, ngx)), dma((2, ngx)),
            dma((nb * ngx * ngy,)), dma((nb * ngx * ngy,)),
        ],
        compiler_params=pltpu.CompilerParams(collective_id=0, has_side_effects=True,
                                             vmem_limit_bytes=60 * 1024 * 1024),
        name="newton_step",
    )(disp, force, kappa, sigma, gap0, pressure, mortar, partner, active)


def solution(mesh):
    placed = (
        P("body", None, "gx", "gy", None),
        P("body", None, "gx", "gy", None),
        P("body", "gx", "gy", None),
        P("body", "gx", "gy", None),
        P(("gx", "gy"), None),
        P(("gx", "gy"), None),
        P(("gx", "gy"), None, None),
        P(("gx", "gy")),
        P(("gx", "gy")),
    )
    return jax.shard_map(
        on_device,
        mesh=mesh,
        in_specs=placed,
        out_specs=(P("body", None, "gx", "gy", None), P(("gx", "gy"), None)),
        check_vma=False,
    )
```

```python
import functools

import jax
import jax.numpy as jnp
from jax import lax
from jax.experimental import pallas as pl
from jax.experimental.pallas import tpu as pltpu
from jax.sharding import PartitionSpec as P

MESH = pl.DeviceIdType.MESH
YB = 8
DIRS = tuple((dx, dy) for dx in (-1, 0, 1) for dy in (-1, 0, 1) if dx != 0 or dy != 0)


def kernel(nb, ngx, ngy, disp, force, kappa, sigma, gap0_in, press_in, mortar, partner_in, active_in,
           inc_out, np_out, gap0, press, partner, active, f0, f1, f2, v2, diag, force_v, sigma_v, mort, surf, usend, urecv,
           final, cols, load_sem, hs, hr, ss, sr, us, ur, fs, fr):
    comp, cx, cy, nz = force_v.shape
    bpd, sblk = gap0.shape
    per = sblk // cy
    b = lax.axis_index("body")
    gx = lax.axis_index("gx")
    gy = lax.axis_index("gy")

    loads = [
        pltpu.make_async_copy(disp.at[0], f0.at[pl.ds(0, comp), pl.ds(1, cx), pl.ds(YB, cy)], load_sem.at[0]),
        pltpu.make_async_copy(kappa.at[0], f0.at[comp, pl.ds(1, cx), pl.ds(YB, cy)], load_sem.at[1]),
        pltpu.make_async_copy(mortar, mort, load_sem.at[2]),
        pltpu.make_async_copy(sigma.at[0], sigma_v, load_sem.at[3]),
        pltpu.make_async_copy(force.at[0], force_v, load_sem.at[4]),
        pltpu.make_async_copy(gap0_in, gap0, load_sem.at[5]),
        pltpu.make_async_copy(press_in, press, load_sem.at[6]),
        pltpu.make_async_copy(partner_in, partner, load_sem.at[7]),
        pltpu.make_async_copy(active_in, active, load_sem.at[8]),
    ]
    for load in loads:
        load.start()

    def exists(dx, dy):
        good = jnp.bool_(True)
        if dx < 0:
            good = good & (gx >= 1)
        if dx > 0:
            good = good & (gx < ngx - 1)
        if dy < 0:
            good = good & (gy >= 1)
        if dy > 0:
            good = good & (gy < ngy - 1)
        return good

    row_peers = [(db, k) for db in range(nb) for k in range(ngx) if db or k]
    count = nb * ngx * ngy
    me = (b * ngx + gx) * ngy + gy

    def place_of(other):
        return {"body": other // (ngx * ngy), "gx": lax.rem(other // ngy, ngx), "gy": lax.rem(other, ngy)}

    def each_peer(act):
        if count <= 64:
            for k in range(1, count):
                act(k)
        else:
            pl.loop(1, count)(act)

    barrier = pltpu.get_barrier_semaphore()
    if ngy <= 4:
        for db, k in row_peers:
            pl.semaphore_signal(barrier, inc=1, device_id={"body": lax.rem(b + db, nb), "gx": lax.rem(gx + k, ngx)},
                                device_id_type=MESH)
        expect = len(row_peers)
        for dx, dy in DIRS:
            if dy:
                here = exists(dx, dy)
                expect = expect + here.astype(jnp.int32)

                @pl.when(here)
                def _():
                    pl.semaphore_signal(barrier, inc=1, device_id={"gx": gx + dx, "gy": gy + dy}, device_id_type=MESH)
    else:
        each_peer(lambda k: pl.semaphore_signal(barrier, inc=1, device_id=place_of(lax.rem(me + k, count)),
                                                device_id_type=MESH))
        expect = count - 1

    for side, x in ((-1, 0), (1, cx + 1)):
        @pl.when(jnp.logical_not(exists(side, 0)))
        def _():
            for f in (f0, f1, f2):
                for c in range(f.shape[0]):
                    f[c, x, YB - 1 : YB] = jnp.zeros((1, nz), f.dtype)
                    f[c, x, YB : YB + cy] = jnp.zeros((cy, nz), f.dtype)
                    f[c, x, YB + cy : YB + cy + 1] = jnp.zeros((1, nz), f.dtype)
    for side, y in ((-1, YB - 1), (1, YB + cy)):
        @pl.when(jnp.logical_not(exists(0, side)))
        def _():
            for f in (f0, f1, f2):
                for c in range(f.shape[0]):
                    for x in range(cx + 2):
                        f[c, x, y : y + 1] = jnp.zeros((1, nz), f.dtype)

    lane = lax.broadcasted_iota(jnp.int32, (sblk, nz), 1)
    eye = lax.broadcasted_iota(jnp.int32, (sblk, nz), 0) == lane
    first_lane = lane == 0
    lane_row = lax.broadcasted_iota(jnp.int32, (cy, nz), 1)
    left_w = jnp.where(lane_row == 0, 0.0, 0.5)
    right_w = jnp.where(lane_row == nz - 1, 0.0, 0.5)

    def to_col(row):
        return jnp.sum(jnp.where(eye, row, 0.0), axis=1, keepdims=True)

    def to_row(col):
        return jnp.sum(jnp.where(eye, col, 0.0), axis=0, keepdims=True)

    def tz(v):
        return v + left_w * pltpu.roll(v, 1, 1) + right_w * pltpu.roll(v, nz - 1, 1)

    def surface_rows(f, r):
        for l in range(bpd):
            block = f[comp - 1, 1 + l * per : 1 + (l + 1) * per, YB : YB + cy, :].reshape(sblk, nz)
            surf[r, b, gx, l : l + 1, :] = to_row(block[:, 0:1])

    pending = []

    def halo_copy(f, r, d, dx, dy, sending):
        def part(delta, size, base):
            if delta == 0:
                return pl.ds(base, size), pl.ds(base, size)
            if delta < 0:
                return pl.ds(base, 1), pl.ds(base + size, 1)
            return pl.ds(base + size - 1, 1), pl.ds(base - 1, 1)
        sx, tx = part(dx, cx, 1)
        sy, ty = part(dy, cy, YB)
        allc = pl.ds(0, f.shape[0])
        return pltpu.make_async_remote_copy(
            src_ref=f.at[allc, sx, sy], dst_ref=f.at[allc, tx, ty], send_sem=hs.at[r, d], recv_sem=hr.at[r, d],
            device_id={"gx": gx + dx, "gy": gy + dy}, device_id_type=MESH)

    def halo_send(f, r):
        for d, (dx, dy) in enumerate(DIRS):
            @pl.when(exists(dx, dy))
            def _():
                halo_copy(f, r, d, dx, dy, True).start()

    def halo_wait(f, r):
        for d, (dx, dy) in enumerate(DIRS):
            @pl.when(exists(-dx, -dy))
            def _():
                halo_copy(f, r, d, dx, dy, False).wait_recv()

    def halo_done(f, r):
        for d, (dx, dy) in enumerate(DIRS):
            @pl.when(exists(dx, dy))
            def _():
                halo_copy(f, r, d, dx, dy, True).wait_send()

    def surf_copy(r, i, db, k, incoming):
        ob, og = lax.rem(b + db, nb), lax.rem(gx + k, ngx)
        wb, wg = (ob, og) if incoming else (b, gx)
        return pltpu.make_async_remote_copy(
            src_ref=surf.at[r, wb, wg], dst_ref=surf.at[r, wb, wg], send_sem=ss.at[r, i],
            recv_sem=sr.at[r, wb * ngx + wg], device_id={"body": ob, "gx": og}, device_id_type=MESH)

    def surf_each(r, incoming, act):
        for i, (db, k) in enumerate(row_peers):
            def go():
                act(surf_copy(r, i, db, k, incoming))
            if db == 1 and k == 0:
                go()
            else:
                origin = lax.rem(b + db, nb) if incoming else b
                pl.when(origin == 1)(go)

    def surf_send(r):
        surf_each(r, False, lambda copy: copy.start())

    def surf_wait(r):
        surf_each(r, True, lambda copy: copy.wait_recv())

    def u_copy(r, k, incoming):
        og = lax.rem(gx + k, ngx)
        return pltpu.make_async_remote_copy(
            src_ref=usend.at[r, og], dst_ref=urecv.at[r, og if incoming else gx], send_sem=us.at[r, k],
            recv_sem=ur.at[r, og if incoming else gx], device_id={"gx": og}, device_id_type=MESH)

    def final_copy(k, incoming):
        other = lax.rem(me + k, count)
        w = other if incoming else me
        return pltpu.make_async_remote_copy(
            src_ref=final.at[w], dst_ref=final.at[w], send_sem=fs.at[k], recv_sem=fr.at[w],
            device_id=place_of(other),
            device_id_type=MESH)

    def b_of(r, l):
        picked = jnp.zeros((1, sblk), jnp.float32)
        for g in range(ngx):
            for q in range(bpd):
                picked = picked + jnp.where(partner[l] == g * bpd + q, surf[r, 1, g, q : q + 1, :], 0.0)
        slave = surf[r, 0, gx, l : l + 1, :]
        return -jnp.sum(mort[l] * picked + jnp.where(eye, slave, 0.0), axis=1, keepdims=True)

    def u_start(r):
        pulled = [jnp.sum(mort[l] * cols[5, l], axis=0, keepdims=True) for l in range(bpd)]
        for g in range(ngx):
            for q in range(bpd):
                row = jnp.zeros((1, sblk), jnp.float32)
                for l in range(bpd):
                    row = row + jnp.where(partner[l] == g * bpd + q, pulled[l], 0.0)
                usend[r, g, q : q + 1, :] = row

        @pl.when(b == 1)
        def _():
            for k in range(1, ngx):
                u_copy(r, k, False).start()

    def u_finish(r, f):
        def add(l, col):
            xs = slice(1 + l * per, 1 + (l + 1) * per)
            block = f[comp - 1, xs, YB : YB + cy, :].reshape(sblk, nz)
            f[comp - 1, xs, YB : YB + cy, :] = (block - jnp.where(first_lane, col, 0.0)).reshape(per, cy, nz)

        @pl.when(b == 0)
        def _():
            for l in range(bpd):
                add(l, cols[5, l])

        @pl.when(b == 1)
        def _():
            for k in range(1, ngx):
                u_copy(r, k, True).wait_recv()
            urecv[r, gx] = usend[r, gx]
            for l in range(bpd):
                row = urecv[r, 0, l : l + 1, :]
                for g in range(1, ngx):
                    row = row + urecv[r, g, l : l + 1, :]
                add(l, to_col(row))

    def apply(f, emit):
        @pl.loop(0, comp)
        def _(c):
            window = []
            for x in range(cx + 2):
                kap = [f0[comp, x, YB + s : YB + s + cy, :] for s in (-1, 0, 1)]
                val = [f[c, x, YB + s : YB + s + cy, :] for s in (-1, 0, 1)]
                window.append((val[1] + 0.5 * (val[0] + val[2]),
                               kap[1] * val[1] + 0.5 * (kap[0] * val[0] + kap[2] * val[2])))
                if x >= 2:
                    p = window[x - 1][0] + 0.5 * (window[x - 2][0] + window[x][0])
                    q = window[x - 1][1] + 0.5 * (window[x - 2][1] + window[x][1])
                    k0 = f0[comp, x - 1, YB : YB + cy, :]
                    v0 = f[c, x - 1, YB : YB + cy, :]
                    emit(c, x - 2, diag[x - 2] * v0 - k0 * tz(p) - tz(q))

    loads[0].wait()
    loads[1].wait()
    surface_rows(f0, 0)
    pl.semaphore_wait(barrier, expect)

    surf_send(0)
    halo_send(f0, 0)
    for load in loads[2:]:
        load.wait()
    surf_wait(0)
    for l in range(bpd):
        gap = to_col(gap0[l : l + 1, :]) + b_of(0, l)
        prs = to_col(press[l : l + 1, :])
        radius = jnp.sqrt(gap * gap + prs * prs + 0.01)
        per_radius = 1.0 / radius
        complement = gap + prs - radius
        per_divisor = 1.0 / ((1.0 - prs * per_radius) + 0.5)
        flag = active[l].astype(jnp.float32)
        cols[1, l] = complement * per_divisor
        cols[2, l] = (1.0 - gap * per_radius) * per_divisor
        cols[5, l] = flag * (prs - complement * per_divisor)
    u_start(0)
    for l in range(bpd):
        cols[0, l] = active[l].astype(jnp.float32) * cols[2, l]
    halo_wait(f0, 0)
    window = []
    for x in range(cx + 2):
        kap = [f0[comp, x, YB + s : YB + s + cy, :] for s in (-1, 0, 1)]
        window.append(kap[1] + 0.5 * (kap[0] + kap[2]))
        if x >= 2:
            p = window[x - 1] + 0.5 * (window[x - 2] + window[x])
            diag[x - 2] = sigma_v[x - 2] + 8.0 * f0[comp, x - 1, YB : YB + cy, :] + tz(p)

    def emit_rhs(c, x, val):
        f1[c, 1 + x, YB : YB + cy, :] = force_v[c, x] - val

    apply(f0, emit_rhs)
    u_finish(0, f1)

    surface_rows(f1, 1)
    surf_send(1)
    halo_send(f1, 1)
    surf_wait(1)
    for l in range(bpd):
        gap = b_of(1, l)
        cols[3, l] = gap
        cols[5, l] = cols[0, l] * gap
    u_start(1)
    halo_wait(f1, 1)

    def emit_v1(c, x, val):
        f2[c, 1 + x, YB : YB + cy, :] = val

    apply(f1, emit_v1)

    def sum_of(left, right):
        total = jnp.zeros((cy, nz), jnp.float32)
        for c in range(comp):
            for x in range(cx):
                total = total + left(c, x) * right(c, x)
        return jnp.sum(jnp.sum(total, axis=0, keepdims=True), axis=1, keepdims=True)

    slave_side = (b == 0).astype(jnp.float32)

    def contact_sum(left, right):
        total = jnp.zeros((1, 1), jnp.float32)
        for l in range(bpd):
            total = total + jnp.sum(cols[0, l] * left(l) * right(l), axis=0, keepdims=True)
        return slave_side * total

    def r0_of(c, x):
        return f1[c, 1 + x, YB : YB + cy, :]

    def v1_of(c, x):
        return f2[c, 1 + x, YB : YB + cy, :]

    u_finish(1, f2)

    surface_rows(f2, 2)
    surf_send(2)
    halo_send(f2, 2)
    rr = sum_of(r0_of, r0_of)
    rv = sum_of(r0_of, v1_of)
    vv = sum_of(v1_of, v1_of)
    own = jnp.where(vv > 0.0, rv / jnp.where(vv > 0.0, vv, 1.0), 0.0)

    def near_of(c, x):
        return r0_of(c, x) - own * v1_of(c, x)

    nn = sum_of(near_of, near_of)
    nv = sum_of(near_of, v1_of)
    surf_wait(2)
    for l in range(bpd):
        cols[4, l] = b_of(2, l)
    halo_wait(f2, 2)

    def emit_v2(c, x, val):
        v2[c, x] = val

    apply(f2, emit_v2)
    nw = sum_of(near_of, lambda c, x: v2[c, x]) + contact_sum(lambda l: cols[3, l] - own * cols[4, l], lambda l: cols[4, l])
    vw = sum_of(v1_of, lambda c, x: v2[c, x]) + contact_sum(lambda l: cols[4, l], lambda l: cols[4, l])

    lane_of = lax.broadcasted_iota(jnp.int32, (1, sblk), 1)
    packed = jnp.zeros((1, sblk), jnp.float32)
    for i, number in enumerate((rr, rv, vv, nn, nv, nw, vw, own)):
        packed = jnp.where(lane_of == i, number, packed)
    final[me] = packed
    each_peer(lambda k: final_copy(k, False).start())
    for r, f in enumerate((f0, f1, f2)):
        halo_done(f, r)
    for r in range(3):
        surf_each(r, False, lambda copy: copy.wait_send())
    @pl.when(b == 1)
    def _():
        for r in range(2):
            for k in range(1, ngx):
                u_copy(r, k, False).wait_send()

    each_peer(lambda k: final_copy(k, True).wait_recv())
    table = final[...].reshape(count, sblk)

    def over(act):
        return jnp.sum(act(*[table[:, i : i + 1] for i in range(8)]), axis=0, keepdims=True)

    norm0 = over(lambda rr, rv, vv, nn, nv, nw, vw, own: rr)
    alpha0 = norm0 / over(lambda rr, rv, vv, nn, nv, nw, vw, own: rv)
    norm1 = over(lambda rr, rv, vv, nn, nv, nw, vw, own: nn - (alpha0 - own) * (2.0 * nv - (alpha0 - own) * vv))
    product1 = over(lambda rr, rv, vv, nn, nv, nw, vw, own:
                    nv - (alpha0 - own) * vv - alpha0 * (nw - (alpha0 - own) * vw))
    ratio = norm1 / norm0
    alpha1 = norm1 / (product1 - ratio * norm1 / alpha0)
    coef_r = alpha0 + alpha1 * (1.0 + ratio)
    coef_v = -alpha1 * alpha0
    for c in range(comp):
        for x in range(cx):
            inc_out[0, c, x] = coef_r * r0_of(c, x) + coef_v * v1_of(c, x)
    for l in range(bpd):
        change = coef_r * cols[3, l] + coef_v * cols[4, l]
        flag = active[l].astype(jnp.float32)
        step = to_row(cols[1, l] + cols[2, l] * change)
        np_out[l : l + 1, :] = flag * (press[l : l + 1, :] - step)
    each_peer(lambda k: final_copy(k, False).wait_send())


def on_device(disp, force, kappa, sigma, gap0, pressure, mortar, partner, active):
    nb, ngx, ngy = (lax.axis_size(a) for a in ("body", "gx", "gy"))
    _, comp, cx, cy, nz = disp.shape
    bpd, sblk, _ = mortar.shape
    f32 = jnp.float32
    any_spec = pl.BlockSpec(memory_space=pl.ANY)
    vmem = pl.BlockSpec(memory_space=pltpu.VMEM)
    rows = cy + 2 * YB
    dma = pltpu.SemaphoreType.DMA
    return pl.pallas_call(
        functools.partial(kernel, nb, ngx, ngy),
        out_shape=(pltpu.VMEM(disp.shape, f32), pltpu.VMEM(gap0.shape, f32)),
        in_specs=[any_spec] * 9,
        out_specs=(vmem, vmem),
        scratch_shapes=[
            pltpu.VMEM((bpd, sblk), f32),
            pltpu.VMEM((bpd, sblk), f32),
            pltpu.SMEM((bpd,), jnp.int32),
            pltpu.SMEM((bpd,), jnp.int32),
            pltpu.VMEM((comp + 1, cx + 2, rows, nz), f32),
            pltpu.VMEM((comp, cx + 2, rows, nz), f32),
            pltpu.VMEM((comp, cx + 2, rows, nz), f32),
            pltpu.VMEM((comp, cx, cy, nz), f32),
            pltpu.VMEM((cx, cy, nz), f32),
            pltpu.VMEM((comp, cx, cy, nz), f32),
            pltpu.VMEM((cx, cy, nz), f32),
            pltpu.VMEM((bpd, sblk, sblk), f32),
            pltpu.VMEM((3, nb, ngx, bpd, sblk), f32),
            pltpu.VMEM((2, ngx, bpd, sblk), f32),
            pltpu.VMEM((2, ngx, bpd, sblk), f32),
            pltpu.VMEM((nb * ngx * ngy, 1, sblk), f32),
            pltpu.VMEM((6, bpd, sblk, 1), f32),
            dma((9,)),
            dma((3, len(DIRS))), dma((3, len(DIRS))),
            dma((3, nb * ngx)), dma((3, nb * ngx)),
            dma((2, ngx)), dma((2, ngx)),
            dma((nb * ngx * ngy,)), dma((nb * ngx * ngy,)),
        ],
        compiler_params=pltpu.CompilerParams(collective_id=0, has_side_effects=True,
                                             vmem_limit_bytes=60 * 1024 * 1024),
        name="newton_step",
    )(disp, force, kappa, sigma, gap0, pressure, mortar, partner, active)


def solution(mesh):
    placed = (
        P("body", None, "gx", "gy", None),
        P("body", None, "gx", "gy", None),
        P("body", "gx", "gy", None),
        P("body", "gx", "gy", None),
        P(("gx", "gy"), None),
        P(("gx", "gy"), None),
        P(("gx", "gy"), None, None),
        P(("gx", "gy")),
        P(("gx", "gy")),
    )
    return jax.shard_map(
        on_device,
        mesh=mesh,
        in_specs=placed,
        out_specs=(P("body", None, "gx", "gy", None), P(("gx", "gy"), None)),
        check_vma=False,
    )
```
